32 devices in a mesh: groups: 2 (over y), ulysses: 4 (over z), blk: 2 (over x), handoff: 2 (over core).
Axes of the slice: x: 2, y: 2, z: 4, core: 2. Of those that a mesh axis runs over, the one named last changes fastest.
Arguments:
- queries: bfloat16 [4, 512, 4096], P(('groups', 'handoff'), ('blk', 'ulysses')), parts along dimension 0, may hold values from -24 to 24
- keys: bfloat16 [4, 512, 2048], P(('groups', 'handoff'), ('blk', 'ulysses')), parts along dimension 0, may hold values from -7.5 to 7.5
- values: bfloat16 [4, 512, 2048], P(('groups', 'handoff'), ('blk', 'ulysses')), parts along dimension 0, may hold values from -6 to 6
- request_pages: int32 [4, 4], P('groups'), parts along dimension 0, may hold values from 1 to 4, 8 in all within a row
- page_table: int32 [4, 8], P('groups'), parts along dimension 0, may hold values from 0 to 15, as said below
Outputs:
- attended: bfloat16 [4, 512, 4096], P(('groups', 'handoff'), ('blk', 'ulysses')), parts along dimension 0
- cache_keys: bfloat16 [32, 16, 64, 128], P(('groups', 'blk', 'handoff'), 'ulysses'), parts along dimension 0
- cache_values: bfloat16 [32, 16, 64, 128], P(('groups', 'blk', 'handoff'), 'ulysses'), parts along dimension 0
The draws below stay inside these ranges and needn't reach their ends.
There are 2 independent parts, one for each index of `groups`. The reference program is written for one: setup_inputs(seed, part) draws one part's arguments, and reference() takes and returns one part's arrays. A program takes and returns all parts, laid end to end along the dimension named above; each array names one. Nothing has to cross between parts.
Inputs may be any that keep to these rules, and one draw needn't show every extreme that they name: `request_pages`: A pack's 4 requests fill its 8 pages; the longest holds exactly 4 of them. `page_table`: all rows together name every pool page once; the 4 pages of each aligned run of 4 pages of a pack's row go in equal numbers to each aligned run of 4 pool pages.
All inputs are finite; a program needn't handle non-finite values.
Results may differ from the reference program's by a relative error of at most 0.012.
Values may be sent and summed in bfloat16 or wider, within the bound.
A program may use at most 64 MiB of HBM per device.

```python
import math
import jax
import jax.numpy as jnp
import numpy as np
from jax import lax

QH = 32
KVH = 16
HD = 128
WINDOW = 4096
PAGE = 64
REQS = 4
SEQ = 512
PACKS = 2
PACK_PAGES = 8
SHARD_PAGES = 4
POOL = 16


def draw_queries(key, part):
    normal = jax.random.normal(jax.random.fold_in(key, 11), (PACKS, SEQ, QH * HD), jnp.float32)
    scaled = normal * 4.0
    return jnp.clip(scaled, -24.0, 24.0).astype(jnp.bfloat16)


def draw_page_table(key, part):
    slots_dev = SHARD_PAGES
    sources = POOL // SHARD_PAGES
    per_peer = slots_dev // sources
    lane_ids = jnp.arange(slots_dev, dtype=jnp.int32)[None, :]
    noise_one = jax.random.randint(jax.random.fold_in(key, 21), (sources, slots_dev), 0, 1 << 20) * slots_dev + lane_ids
    noise_two = jax.random.randint(jax.random.fold_in(key, 22), (sources, slots_dev), 0, 1 << 20) * slots_dev + lane_ids
    first_perm = jnp.argsort(noise_one, axis=1).astype(jnp.int32)
    second_perm = jnp.argsort(noise_two, axis=1).astype(jnp.int32)
    target = first_perm // per_peer
    within = first_perm % per_peer
    source_ids = jnp.arange(sources, dtype=jnp.int32)[:, None]
    slot_index = second_perm[target, source_ids * per_peer + within]
    pool_page = target * slots_dev + slot_index
    blk_lanes = sources // PACKS
    return jnp.transpose(pool_page.reshape(blk_lanes, PACKS, slots_dev), (1, 0, 2)).reshape(PACKS, PACK_PAGES).astype(jnp.int32)


def levels(stream_key, extent, shards, smallest, largest):
    def one(position, shards_of):
        heights = jax.random.uniform(jax.random.fold_in(jax.random.fold_in(stream_key, 6), position), (shards_of,), jnp.float32, smallest / len(shards), largest / len(shards))
        return jnp.repeat(jnp.exp(heights), extent[position] // shards_of).reshape((-1,) + (1,) * (len(extent) - position - 1))

    gain = one(*shards[0])
    for cut in shards[1:]:
        gain = gain * one(*cut)
    return gain


def split_up(count, total, most, skew):
    portions = [(1 << 20) // math.isqrt(standing ** skew) + 1 for standing in range(2, count + 1)]
    surplus, holding = total - most - (count - 1), [1] * (count - 1)
    while surplus > 0:
        movable = [i for i in range(count - 1) if holding[i] < most]
        pool, budget = sum([portions[i] for i in movable]), surplus
        for i in movable:
            extra = min(most - holding[i], max(1, budget * portions[i] // pool), surplus)
            holding[i] = holding[i] + extra
            surplus = surplus - extra
    return np.array([most] + holding)


def ragged(own_key, amount, total, limit, slope):
    if amount == 2:
        one = jax.random.randint(own_key, (), max(1, total - limit), min(limit, total - 1) + 1)
        return jnp.stack([one, total - one])
    lengths = jnp.asarray(split_up(amount, total, limit, slope), jnp.int32)
    twos = (amount - 1) // 2
    giver, receiver = lengths[1:1 + 2 * twos:2], lengths[2:2 + 2 * twos:2]
    slack = jnp.minimum(giver - 1, limit - receiver)
    moved = jax.random.randint(jax.random.fold_in(own_key, 1), (twos,), 0, 1 << 20) % (slack + 1)
    lengths = lengths.at[1:1 + 2 * twos:2].set(giver - moved).at[2:2 + 2 * twos:2].set(receiver + moved)
    return lengths[jax.random.permutation(jax.random.fold_in(own_key, 2), amount)]


def scatter_about(stream_key, dims, width, limit, pieces=(), kind=jnp.bfloat16):
    level = levels(stream_key, dims, pieces, -0.22, 0.18) if pieces else 1.0
    array = jax.random.normal(stream_key, dims, jnp.float32) * width * level
    return jnp.minimum(jnp.maximum(array, -limit), limit).astype(kind)


def setup_inputs(seed: int = 0, part: int = 0) -> dict:
    key_list = jax.random.split(jax.random.key(seed), 6)
    part_splits = jax.random.split(jax.random.fold_in(key_list[5], part), 6)
    queries = draw_queries(jax.random.fold_in(jax.random.fold_in(key_list[5], part), 71), part)
    keys = scatter_about(part_splits[1], (PACKS, SEQ, KVH * HD), 1.25, 7.5, ((0, 2), (1, 8)))
    values = scatter_about(part_splits[2], (PACKS, SEQ, KVH * HD), 1.0, 6.0, ((0, 2), (1, 8)))
    request_pages = jax.vmap(lambda own: ragged(own, REQS, PACK_PAGES, PACK_PAGES // 2, 1))(jax.random.split(part_splits[3], PACKS)).reshape((PACKS, REQS)).astype(jnp.int32)
    page_table = draw_page_table(jax.random.fold_in(jax.random.fold_in(key_list[5], part), 71), part)
    return dict(queries=queries, keys=keys, values=values, request_pages=request_pages, page_table=page_table)


QUERY_SCALE = 144.0 ** -0.5
SOFT_CAP = 50.0
ROPE_BASE = 10000.0


def request_marks(pages_row, positions):
    request_ends = jnp.cumsum(pages_row, dtype=jnp.int32) * PAGE
    request_starts = request_ends - pages_row * PAGE
    owner_index = jnp.sum((positions[:, None] >= request_ends[None, :]).astype(jnp.int32), axis=1)
    first_token = jnp.max(jnp.where(positions[:, None] >= request_starts[None, :], request_starts[None, :], 0), axis=1)
    return owner_index.astype(jnp.int32), (positions - first_token).astype(jnp.int32)


def rotate(head_rows, offsets):
    head_width = head_rows.shape[-1]
    half_width = head_width // 2
    frequency = ROPE_BASE ** (-(2.0 * jnp.arange(half_width, dtype=jnp.float32)) / head_width)
    angles = offsets.astype(jnp.float32)[:, None] * frequency[None, :]
    cosine = jnp.cos(angles)[:, None, :]
    sines = jnp.sin(angles)[:, None, :]
    as_float = head_rows.astype(jnp.float32)
    front_half = as_float[..., :half_width]
    back_half = as_float[..., half_width:]
    turned = jnp.concatenate([front_half * cosine - back_half * sines, back_half * cosine + front_half * sines], axis=-1)
    return turned.astype(jnp.bfloat16)


def reference(queries, keys, values, request_pages, page_table):
    group_size = QH // KVH
    block_rows = math.gcd(SEQ, 512)
    key_span = WINDOW + block_rows
    positions = jnp.arange(SEQ, dtype=jnp.int32)
    pad_positions = jnp.arange(SEQ + WINDOW, dtype=jnp.int32) - WINDOW
    outputs = []
    key_pages = []
    value_pages = []
    for pack_index in range(PACKS):
        owner_all, offsets = request_marks(request_pages[pack_index], positions)
        pad_owner, unused_offsets = request_marks(request_pages[pack_index], pad_positions)
        query_turned = rotate(queries[pack_index].reshape(SEQ, QH, HD), offsets)
        key_turned = rotate(keys[pack_index].reshape(SEQ, KVH, HD), offsets)
        value_heads = values[pack_index].reshape(SEQ, KVH, HD)
        pad_keys = jnp.concatenate([jnp.zeros((WINDOW, KVH, HD), jnp.bfloat16), key_turned], axis=0)
        pad_values = jnp.concatenate([jnp.zeros((WINDOW, KVH, HD), jnp.bfloat16), value_heads], axis=0)

        def attend(offset):
            query_block = lax.dynamic_slice_in_dim(query_turned, offset, block_rows, 0).astype(jnp.float32)
            query_block = query_block.reshape(block_rows, KVH, group_size, HD)
            key_block = lax.dynamic_slice_in_dim(pad_keys, offset, key_span, 0).astype(jnp.float32)
            value_block = lax.dynamic_slice_in_dim(pad_values, offset, key_span, 0).astype(jnp.float32)
            scores = jnp.einsum("qgrd,kgd->gqrk", query_block, key_block, precision=lax.Precision.HIGHEST) * QUERY_SCALE
            capped = SOFT_CAP * jnp.tanh(scores / SOFT_CAP)
            query_pos = lax.dynamic_slice_in_dim(positions, offset, block_rows)
            query_owner = lax.dynamic_slice_in_dim(owner_all, offset, block_rows)
            key_pos = lax.dynamic_slice_in_dim(pad_positions, offset, key_span)
            key_owner = lax.dynamic_slice_in_dim(pad_owner, offset, key_span)
            distance = query_pos[:, None] - key_pos[None, :]
            allowed = (query_owner[:, None] == key_owner[None, :]) & (distance >= 0) & (distance < WINDOW) & (key_pos[None, :] >= 0)
            weights = jnp.where(allowed[None, :, None, :], jnp.exp(capped), jnp.float32(0.0))
            totals = jnp.sum(weights, axis=-1)
            rounded = lax.optimization_barrier(weights.astype(jnp.bfloat16)).astype(jnp.float32)
            mixture = jnp.einsum("gqrk,kgd->qgrd", rounded, value_block, precision=lax.Precision.HIGHEST)
            return (mixture / jnp.transpose(totals, (1, 0, 2))[..., None]).astype(jnp.bfloat16)

        starts = jnp.arange(SEQ // block_rows, dtype=jnp.int32) * block_rows
        blocks = lax.map(attend, starts)
        outputs.append(blocks.reshape(SEQ, QH * HD))
        key_pages.append(key_turned.reshape(PACK_PAGES, PAGE, KVH, HD))
        value_pages.append(value_heads.reshape(PACK_PAGES, PAGE, KVH, HD))
    attended = jnp.stack(outputs)
    flat_keys = jnp.transpose(jnp.concatenate(key_pages, axis=0), (0, 2, 1, 3))
    flat_values = jnp.transpose(jnp.concatenate(value_pages, axis=0), (0, 2, 1, 3))
    pool_slots = page_table.reshape(-1).astype(jnp.int32)
    cache_keys = jnp.zeros_like(flat_keys).at[pool_slots].set(flat_keys)
    cache_values = jnp.zeros_like(flat_values).at[pool_slots].set(flat_values)
    return attended, cache_keys, cache_values
```

```python
import math

import jax
import jax.numpy as jnp
from jax import lax
from jax.sharding import PartitionSpec as P

QH = 32
KVH = 16
HD = 128
WINDOW = 4096
PAGE = 64


QUERY_SCALE = 144.0 ** (-0.5)
SOFT_CAP = 50.0
ROPE_BASE = 10000.0


def from_behind(block, axis, distance):
    devices = range(lax.axis_size(axis))
    route = [(i - distance, i) for i in devices if i - distance in devices]
    return lax.ppermute(block, axis, route)


def request_marks(pages_row, positions):
    request_ends = jnp.cumsum(pages_row, dtype=jnp.int32) * PAGE
    request_starts = request_ends - pages_row * PAGE
    owner_index = jnp.sum((positions[:, None] >= request_ends[None, :]).astype(jnp.int32), axis=1)
    first_token = jnp.max(
        jnp.where(positions[:, None] >= request_starts[None, :], request_starts[None, :], 0), axis=1
    )
    return (owner_index, positions - first_token)


def rotate(head_rows, offsets):
    head_width = head_rows.shape[-1]
    half_width = head_width // 2
    frequency = ROPE_BASE ** (-(2.0 * jnp.arange(half_width, dtype=jnp.float32)) / head_width)
    angles = offsets.astype(jnp.float32)[:, None] * frequency[None, :]
    cosine = jnp.cos(angles)[:, None, :]
    sines = jnp.sin(angles)[:, None, :]
    as_float = head_rows.astype(jnp.float32)
    front_half = as_float[..., :half_width]
    back_half = as_float[..., half_width:]
    turned = jnp.concatenate(
        [front_half * cosine - back_half * sines, back_half * cosine + front_half * sines], axis=-1
    )
    return turned.astype(jnp.bfloat16)


def body(queries, keys, values, request_pages, page_table):
    local_rows = queries.shape[1]
    ulysses_size = lax.axis_size("ulysses")
    blk_size = lax.axis_size("blk")
    core_count = lax.axis_size("handoff")
    pack_index = lax.axis_index("handoff")
    blk_index = lax.axis_index("blk")
    shard_rows = local_rows * ulysses_size
    window = min(WINDOW, page_table.shape[1] // 2 * PAGE)
    earlier_count = min(window // shard_rows, blk_size - 1)
    kv_local = KVH // ulysses_size
    group_size = QH // KVH
    query_split = queries[0].reshape(local_rows, ulysses_size, kv_local * group_size * HD)
    key_split = keys[0].reshape(local_rows, ulysses_size, kv_local * HD)
    value_split = values[0].reshape(local_rows, ulysses_size, kv_local * HD)
    pages_row = lax.dynamic_index_in_dim(request_pages, pack_index, 0, keepdims=False)
    positions = blk_index * shard_rows + jnp.arange(shard_rows, dtype=jnp.int32)
    query_owner, offsets = request_marks(pages_row, positions)
    queries_moved, keys_moved, values_moved = (
        lax.all_to_all(query_split, "ulysses", split_axis=1, concat_axis=0, tiled=True),
        lax.all_to_all(key_split, "ulysses", split_axis=1, concat_axis=0, tiled=True),
        lax.all_to_all(value_split, "ulysses", split_axis=1, concat_axis=0, tiled=True),
    )
    key_turned = rotate(keys_moved.reshape(shard_rows, kv_local, HD), offsets)
    local_kv = jnp.stack(
        [
            key_turned.reshape(shard_rows, kv_local * HD),
            values_moved.reshape(shard_rows, kv_local * HD),
        ]
    )
    earlier = []
    carried = local_kv
    for hop in range(earlier_count):
        carried = from_behind(carried, "blk", 1)
        earlier.append(carried)
    slots_dev = shard_rows // PAGE
    sources = blk_size * core_count
    per_peer = slots_dev // sources
    pack_row = lax.dynamic_index_in_dim(page_table, pack_index, 0, keepdims=False)
    my_pages = lax.dynamic_slice_in_dim(pack_row, blk_index * slots_dev, slots_dev)
    send_order = jnp.argsort(my_pages)
    paged = local_kv.reshape(2, slots_dev, PAGE, kv_local, HD)[:, send_order]
    paged = jnp.transpose(paged, (0, 1, 3, 2, 4))
    outgoing = paged.reshape(2, sources, per_peer, kv_local, PAGE, HD)
    received = lax.all_to_all(outgoing, ("blk", "handoff"), split_axis=1, concat_axis=1, tiled=True)
    received = received.reshape(2, slots_dev, kv_local, PAGE, HD)
    page_grid = jnp.transpose(
        page_table.reshape(core_count, blk_size, slots_dev), (1, 0, 2)
    ).reshape(sources, slots_dev)
    my_index = blk_index * core_count + pack_index
    is_here = page_grid // slots_dev == my_index
    picked = (
        jnp.sort(jnp.where(is_here, page_grid, page_table.size), axis=1)[:, :per_peer]
        - my_index * slots_dev
    )
    inverse = jnp.argsort(picked.reshape(-1))
    cache_keys = received[0][inverse]
    cache_values = received[1][inverse]
    query_turned = rotate(queries_moved.reshape(shard_rows, kv_local * group_size, HD), offsets)
    query_turned = query_turned.reshape(shard_rows, kv_local, group_size, HD)
    front_rows = window - earlier_count * shard_rows
    front_zeros = jnp.zeros((2, front_rows, kv_local * HD), jnp.bfloat16)
    table_kv = jnp.concatenate([front_zeros] + earlier[::-1] + [local_kv], axis=1)
    key_positions = (
        blk_index * shard_rows - window + jnp.arange(window + shard_rows, dtype=jnp.int32)
    )
    key_owner, unused_offsets = request_marks(pages_row, key_positions)
    block_rows = math.gcd(shard_rows, 128)
    key_span = window + block_rows

    def attend(offset):
        query_block = lax.dynamic_slice_in_dim(query_turned, offset, block_rows, 0)
        kv_block = lax.dynamic_slice_in_dim(table_kv, offset, key_span, 1)
        key_block = kv_block[0].reshape(key_span, kv_local, HD)
        value_block = kv_block[1].reshape(key_span, kv_local, HD)
        scores = (
            jnp.einsum("qgrd,kgd->gqrk", query_block, key_block, preferred_element_type=jnp.float32)
            * QUERY_SCALE
        )
        capped = SOFT_CAP * jnp.tanh(scores / SOFT_CAP)
        query_pos = lax.dynamic_slice_in_dim(positions, offset, block_rows)
        query_part = lax.dynamic_slice_in_dim(query_owner, offset, block_rows)
        key_pos = lax.dynamic_slice_in_dim(key_positions, offset, key_span)
        key_part = lax.dynamic_slice_in_dim(key_owner, offset, key_span)
        distance = query_pos[:, None] - key_pos[None, :]
        allowed = (
            (query_part[:, None] == key_part[None, :])
            & (distance >= 0)
            & (distance < window)
            & (key_pos[None, :] >= 0)
        )
        weights = jnp.where(allowed[None, :, None, :], jnp.exp(capped), jnp.float32(0.0))
        totals = jnp.sum(weights, axis=-1)
        mixture = jnp.einsum(
            "gqrk,kgd->qgrd",
            weights.astype(jnp.bfloat16),
            value_block,
            preferred_element_type=jnp.float32,
        )
        return (mixture / jnp.transpose(totals, (1, 0, 2))[..., None]).astype(jnp.bfloat16)

    starts = jnp.arange(shard_rows // block_rows, dtype=jnp.int32) * block_rows
    blocks = lax.map(attend, starts)
    outgoing_heads = blocks.reshape(ulysses_size, local_rows, 1, kv_local * group_size * HD)
    merged = lax.all_to_all(outgoing_heads, "ulysses", split_axis=0, concat_axis=2, tiled=True)
    attended = merged.reshape(1, local_rows, QH * HD)
    return (attended, cache_keys, cache_values)


def solution(mesh):
    in_specs = (
        P(("groups", "handoff"), ("blk", "ulysses"), None),
        P(("groups", "handoff"), ("blk", "ulysses"), None),
        P(("groups", "handoff"), ("blk", "ulysses"), None),
        P("groups", None),
        P("groups", None),
    )
    out_specs = (
        P(("groups", "handoff"), ("blk", "ulysses"), None),
        P(("groups", "blk", "handoff"), "ulysses", None, None),
        P(("groups", "blk", "handoff"), "ulysses", None, None),
    )
    return jax.shard_map(body, mesh=mesh, in_specs=in_specs, out_specs=out_specs, check_vma=False)
```

```python
import functools

import jax
import jax.numpy as jnp
import numpy as np
from jax import lax
from jax.experimental import pallas as pl
from jax.experimental.pallas import tpu as pltpu
from jax.sharding import PartitionSpec as P

QH = 32
KVH = 16
HD = 128
WINDOW = 4096
PAGE = 64

QUERY_SCALE = 144.0 ** (-0.5)
SOFT_CAP = 50.0
ROPE_BASE = 10000.0
MESH = pl.DeviceIdType.MESH


def turn(x, cosine, sine):
    wide = x.astype(jnp.float32)
    return (wide * cosine + pltpu.roll(wide, HD // 2, 1) * sine).astype(jnp.bfloat16)


def pick(index, choices):
    chosen = choices[0]
    for j in range(1, len(choices)):
        chosen = jnp.where(index == j, choices[j], chosen)
    return chosen


def kernel(
    sizes, q_ref, k_ref, v_ref, freq_ref, pages_ref, table_ref,
    out_ref, ck_ref, cv_ref,
    kraw, tab_k, tab_v, qbuf, obuf, cos_t, sin_t, out_k, out_v, got_k, got_v,
    in_send, in_recv, in_local, x_send, x_recv, c_send, c_recv, c_local, o_send, o_recv, o_local,
):
    ulysses, blks, cores, local, kvl, group, reach, reqs = sizes
    rows = ulysses * local
    slots = rows // PAGE
    sources = blks * cores
    back = min(-(-reach // rows), blks - 1)
    home = back * rows
    qw = group * HD
    me = lax.axis_index("ulysses")
    blk = lax.axis_index("blk")
    pack = lax.axis_index("handoff")
    mine = blk * cores + pack

    barrier = pltpu.get_barrier_semaphore()

    def u_peer(i):
        return lax.rem(me + i, ulysses)

    def s_peer(i):
        p = lax.rem(mine + i, sources)
        return p, {"blk": p // cores, "handoff": lax.rem(p, cores)}

    for i in range(1, ulysses):
        pl.semaphore_signal(barrier, inc=1, device_id={"ulysses": u_peer(i)}, device_id_type=MESH)
    for i in range(1, sources):
        pl.semaphore_signal(barrier, inc=1, device_id=s_peer(i)[1], device_id_type=MESH)

    for hop in range(1, back + 1):
        @pl.when(blk < hop)
        def _():
            part = pl.ds((back - hop) * rows, rows)
            tab_k[:, part, :] = jnp.zeros((kvl, rows, HD), jnp.bfloat16)
            tab_v[:, part, :] = jnp.zeros((kvl, rows, HD), jnp.bfloat16)

    pl.semaphore_wait(barrier, ulysses - 1 + sources - 1)

    def landing(what, h, whose):
        if what == 0:
            return kraw.at[h, pl.ds(whose * local, local), :]
        if what == 1:
            return tab_v.at[h, pl.ds(home + whose * local, local), :]
        return qbuf.at[h, pl.ds(whose * local, local), :]

    def leaving(what, h, whose):
        width = qw if what == 2 else HD
        ref = (k_ref, v_ref, q_ref)[what]
        return ref.at[:, pl.ds(pl.multiple_of((whose * kvl + h) * width, width), width)]

    def incoming(what, h, i):
        return pltpu.make_async_remote_copy(
            src_ref=leaving(what, h, u_peer(i)), dst_ref=landing(what, h, me),
            send_sem=in_send.at[what, h, i - 1], recv_sem=in_recv.at[what, h, i - 1],
            device_id={"ulysses": u_peer(i)}, device_id_type=MESH,
        )

    def own_in(what, h):
        return pltpu.make_async_copy(leaving(what, h, me), landing(what, h, me), in_local.at[what, h])

    order = [(w, h) for h in range(kvl) for w in (0, 1)] + [(2, h) for h in range(kvl)]
    for what, h in order:
        for i in range(1, ulysses):
            incoming(what, h, i).start()
        own_in(what, h).start()

    def arrive(what, h):
        own_in(what, h).wait()
        for i in range(1, ulysses):
            incoming(what, h, i).wait_recv()

    ends = []
    starts = []
    total = jnp.int32(0)
    for r in range(reqs):
        starts.append(total)
        total = total + pages_ref[pack, r] * PAGE
        ends.append(total)

    def first_token(pos):
        first = jnp.zeros_like(pos)
        for r in range(reqs):
            first = jnp.maximum(first, jnp.where(pos >= starts[r], starts[r], 0))
        return first

    pos_rows = blk * rows + lax.broadcasted_iota(jnp.int32, (rows, HD), 0)
    rel = (pos_rows - first_token(pos_rows)).astype(jnp.float32)
    angles = rel * freq_ref[...]
    lanes = lax.broadcasted_iota(jnp.int32, (rows, HD), 1)
    cos_t[...] = jnp.cos(angles)
    sine = jnp.sin(angles)
    sin_t[...] = jnp.where(lanes < HD // 2, -sine, sine)

    def onward(which, h, hop):
        tab = (tab_k, tab_v)[which]
        return pltpu.make_async_remote_copy(
            src_ref=tab.at[h, pl.ds(home, rows), :],
            dst_ref=tab.at[h, pl.ds((back - hop) * rows, rows), :],
            send_sem=x_send.at[which, h, hop - 1], recv_sem=x_recv.at[which, h, hop - 1],
            device_id={"blk": lax.rem(blk + hop, blks)}, device_id_type=MESH,
        )

    for h in range(kvl):
        arrive(0, h)
        tab_k[h, pl.ds(home, rows), :] = turn(kraw[h], cos_t[...], sin_t[...])
        arrive(1, h)
        for hop in range(1, back + 1):
            @pl.when(blk + hop < blks)
            def _():
                onward(0, h, hop).start()
                onward(1, h, hop).start()

    def page_for(owner):
        def step(j, found):
            page = table_ref[pack, blk * slots + j]
            return found + jnp.where(lax.div(page, jnp.int32(slots)) == owner, j, 0)
        return lax.fori_loop(0, slots, step, jnp.int32(0))

    def handed(which, i):
        src, dst = ((out_k, got_k), (out_v, got_v))[which]
        return pltpu.make_async_remote_copy(
            src_ref=src.at[i], dst_ref=dst.at[mine],
            send_sem=c_send.at[which, i - 1], recv_sem=c_recv.at[which, i - 1],
            device_id=s_peer(i)[1], device_id_type=MESH,
        )

    def own_page(which):
        src, dst = ((out_k, got_k), (out_v, got_v))[which]
        return pltpu.make_async_copy(src.at[0], dst.at[mine], c_local.at[which])

    for i in range(sources):
        chosen = page_for(s_peer(i)[0])
        for tab, out in ((tab_k, out_k), (tab_v, out_v)):
            out[i] = pick(chosen, [tab[:, home + j * PAGE:home + (j + 1) * PAGE, :] for j in range(slots)])
    for i in range(1, sources):
        handed(0, i).start()
        handed(1, i).start()
    own_page(0).start()
    own_page(1).start()

    block = min(rows, 128)
    lead = min(-(-reach // block) * block, home)
    span = lead + block
    chunk = span if span <= 512 else block
    factor = QUERY_SCALE / SOFT_CAP

    def attend(h, i):
        at = i * block
        if not isinstance(i, int):
            at = pl.multiple_of(at, block)
        here = pl.ds(at, block)
        cosine, sine_here = cos_t[here, :], sin_t[here, :]
        query = jnp.concatenate(
            [turn(qbuf[h, here, g * HD:(g + 1) * HD], cosine, sine_here) for g in range(group)], axis=0
        )
        pos = blk * rows + at + lax.broadcasted_iota(jnp.int32, (block, 1), 0)
        low = jnp.maximum(first_token(pos), pos - (WINDOW - 1))
        pos = jnp.concatenate([pos] * group, axis=0)
        low = jnp.concatenate([low] * group, axis=0)
        begin = home + at - lead

        def part(c):
            start = begin + c * chunk
            if not isinstance(start, int):
                start = pl.multiple_of(start, block)
            seen = pl.ds(start, chunk)
            scores = lax.dot_general(
                query, tab_k[h, seen, :], (((1,), (1,)), ((), ())), preferred_element_type=jnp.float32
            )
            weights = jnp.exp(SOFT_CAP * jnp.tanh(scores * factor))
            key_pos = (blk - back) * rows + start + lax.broadcasted_iota(jnp.int32, (1, chunk), 1)
            weights = jnp.where((key_pos <= pos) & (key_pos >= low), weights, 0.0)
            total = jnp.sum(weights, axis=1, keepdims=True)
            mixed = jnp.dot(
                weights.astype(jnp.bfloat16), tab_v[h, seen, :], preferred_element_type=jnp.float32
            )
            return mixed, total

        if span == chunk:
            mixed, total = part(0)
        else:
            def step(c, carry):
                mixed, total = part(c)
                return carry[0] + mixed, carry[1] + total
            mixed, total = lax.fori_loop(
                0, span // chunk, step,
                (jnp.zeros((group * block, HD), jnp.float32), jnp.zeros((group * block, 1), jnp.float32)),
            )
        result = (mixed / total).astype(jnp.bfloat16)
        for g in range(group):
            obuf[h, here, g * HD:(g + 1) * HD] = result[g * block:(g + 1) * block]

    def outgoing(h, i):
        return pltpu.make_async_remote_copy(
            src_ref=obuf.at[h, pl.ds(pl.multiple_of(u_peer(i) * local, local), local), :],
            dst_ref=out_ref.at[:, pl.ds(pl.multiple_of((me * kvl + h) * qw, qw), qw)],
            send_sem=o_send.at[h, i - 1], recv_sem=o_recv.at[h, i - 1],
            device_id={"ulysses": u_peer(i)}, device_id_type=MESH,
        )

    def own_out(h):
        return pltpu.make_async_copy(
            obuf.at[h, pl.ds(pl.multiple_of(me * local, local), local), :],
            out_ref.at[:, pl.ds(pl.multiple_of((me * kvl + h) * qw, qw), qw)],
            o_local.at[h],
        )

    for h in range(kvl):
        for hop in range(1, back + 1):
            @pl.when(blk >= hop)
            def _():
                onward(0, h, hop).wait_recv()
                onward(1, h, hop).wait_recv()
        arrive(2, h)
        if rows // block <= 4:
            for i in range(rows // block):
                attend(h, i)
        else:
            def each(i, carry):
                attend(h, i)
                return carry
            lax.fori_loop(0, rows // block, each, 0)
        for i in range(1, ulysses):
            outgoing(h, i).start()
        own_out(h).start()

    own_page(0).wait()
    own_page(1).wait()
    for i in range(1, sources):
        handed(0, i).wait_recv()
        handed(1, i).wait_recv()
    for j in range(slots):
        def step(n, found, j=j):
            s = n // slots
            page = table_ref[lax.rem(s, cores), (s // cores) * slots + lax.rem(n, slots)]
            return found + jnp.where(page == mine * slots + j, s, 0)
        source = lax.fori_loop(0, sources * slots, step, jnp.int32(0))
        ck_ref[j] = pick(source, [got_k[s] for s in range(sources)])
        cv_ref[j] = pick(source, [got_v[s] for s in range(sources)])

    for i in range(1, sources):
        handed(0, i).wait_send()
        handed(1, i).wait_send()
    for what, h in order:
        for i in range(1, ulysses):
            incoming(what, h, i).wait_send()
    for h in range(kvl):
        for hop in range(1, back + 1):
            @pl.when(blk + hop < blks)
            def _():
                onward(0, h, hop).wait_send()
                onward(1, h, hop).wait_send()
    for h in range(kvl):
        own_out(h).wait()
        for i in range(1, ulysses):
            outgoing(h, i).wait()


def body(queries, keys, values, request_pages, page_table):
    local = queries.shape[1]
    ulysses = lax.axis_size("ulysses")
    blks = lax.axis_size("blk")
    cores = lax.axis_size("handoff")
    kvl = KVH // ulysses
    group = QH // KVH
    rows = local * ulysses
    slots = rows // PAGE
    sources = blks * cores
    assert slots == sources
    reach = min(WINDOW, page_table.shape[1] // 2 * PAGE)
    back = min(-(-reach // rows), blks - 1)
    reqs = request_pages.shape[1]
    half = np.arange(HD // 2, dtype=np.float64)
    freq = (ROPE_BASE ** (-2.0 * half / HD)).astype(np.float32)
    freq = jnp.asarray(np.concatenate([freq, freq])[None, :])
    sizes = (ulysses, blks, cores, local, kvl, group, reach, reqs)
    qw = group * HD
    bf = jnp.bfloat16
    dma = pltpu.SemaphoreType.DMA
    hops = max(back, 1)
    anywhere = pl.BlockSpec(memory_space=pl.ANY)
    vmem = pl.BlockSpec(memory_space=pltpu.VMEM)
    smem = pl.BlockSpec(memory_space=pltpu.SMEM)
    attended, cache_keys, cache_values = pl.pallas_call(
        functools.partial(kernel, sizes),
        out_shape=(
            jax.ShapeDtypeStruct((local, QH * HD), bf),
            jax.ShapeDtypeStruct((slots, kvl, PAGE, HD), bf),
            jax.ShapeDtypeStruct((slots, kvl, PAGE, HD), bf),
        ),
        in_specs=[anywhere, anywhere, anywhere, vmem, smem, smem],
        out_specs=(anywhere, vmem, vmem),
        scratch_shapes=[
            pltpu.VMEM((kvl, rows, HD), bf),
            pltpu.VMEM((kvl, (back + 1) * rows, HD), bf),
            pltpu.VMEM((kvl, (back + 1) * rows, HD), bf),
            pltpu.VMEM((kvl, rows, qw), bf),
            pltpu.VMEM((kvl, rows, qw), bf),
            pltpu.VMEM((rows, HD), jnp.float32),
            pltpu.VMEM((rows, HD), jnp.float32),
            pltpu.VMEM((sources, kvl, PAGE, HD), bf),
            pltpu.VMEM((sources, kvl, PAGE, HD), bf),
            pltpu.VMEM((sources, kvl, PAGE, HD), bf),
            pltpu.VMEM((sources, kvl, PAGE, HD), bf),
            dma((3, kvl, ulysses - 1)),
            dma((3, kvl, ulysses - 1)),
            dma((3, kvl)),
            dma((2, kvl, hops)),
            dma((2, kvl, hops)),
            dma((2, sources - 1)),
            dma((2, sources - 1)),
            dma((2,)),
            dma((kvl, ulysses - 1)),
            dma((kvl, ulysses - 1)),
            dma((kvl,)),
        ],
        compiler_params=pltpu.CompilerParams(collective_id=0, has_side_effects=True),
    )(queries[0], keys[0], values[0], freq, request_pages, page_table)
    return (attended[None], cache_keys, cache_values)


def solution(mesh):
    in_specs = (
        P(("groups", "handoff"), ("blk", "ulysses"), None),
        P(("groups", "handoff"), ("blk", "ulysses"), None),
        P(("groups", "handoff"), ("blk", "ulysses"), None),
        P("groups", None),
        P("groups", None),
    )
    out_specs = (
        P(("groups", "handoff"), ("blk", "ulysses"), None),
        P(("groups", "blk", "handoff"), "ulysses", None, None),
        P(("groups", "blk", "handoff"), "ulysses", None, None),
    )
    return jax.shard_map(body, mesh=mesh, in_specs=in_specs, out_specs=out_specs, check_vma=False)
```

```python
import functools

import jax
import jax.numpy as jnp
import numpy as np
from jax import lax
from jax.experimental import pallas as pl
from jax.experimental.pallas import tpu as pltpu
from jax.sharding import PartitionSpec as P

QH = 32
KVH = 16
HD = 128
WINDOW = 4096
PAGE = 64

QUERY_SCALE = 144.0 ** (-0.5)
SOFT_CAP = 50.0
ROPE_BASE = 10000.0
MESH = pl.DeviceIdType.MESH


def turn(x, cosine, sine):
    wide = x.astype(jnp.float32)
    return (wide * cosine + pltpu.roll(wide, HD // 2, 1) * sine).astype(jnp.bfloat16)


def pick(index, choices):
    chosen = choices[0]
    for j in range(1, len(choices)):
        chosen = jnp.where(index == j, choices[j], chosen)
    return chosen


def kernel(
    sizes, q_ref, k_ref, v_ref, freq_ref, pages_ref, table_ref,
    out_ref, got_k, got_v,
    kraw, tab_k, tab_v, qbuf, obuf, cos_t, sin_t, out_k, out_v,
    in_send, in_recv, in_local, x_send, x_recv, c_send, c_recv, c_local, o_send, o_recv, o_local,
):
    ulysses, blks, cores, local, kvl, group, reach, reqs = sizes
    rows = ulysses * local
    slots = rows // PAGE
    sources = blks * cores
    back = min(-(-reach // rows), blks - 1)
    home = back * rows
    qw = group * HD
    me = lax.axis_index("ulysses")
    blk = lax.axis_index("blk")
    pack = lax.axis_index("handoff")
    mine = blk * cores + pack

    barrier = pltpu.get_barrier_semaphore()

    def u_peer(i):
        return lax.rem(me + i, ulysses)

    def s_peer(i):
        p = lax.rem(mine + i, sources)
        return p, {"blk": p // cores, "handoff": lax.rem(p, cores)}

    for i in range(1, ulysses):
        pl.semaphore_signal(barrier, inc=1, device_id={"ulysses": u_peer(i)}, device_id_type=MESH)
    for i in range(1, sources):
        pl.semaphore_signal(barrier, inc=1, device_id=s_peer(i)[1], device_id_type=MESH)

    for hop in range(1, back + 1):
        @pl.when(blk < hop)
        def _():
            part = pl.ds((back - hop) * rows, rows)
            tab_k[:, part, :] = jnp.zeros((kvl, rows, HD), jnp.bfloat16)
            tab_v[:, part, :] = jnp.zeros((kvl, rows, HD), jnp.bfloat16)

    pl.semaphore_wait(barrier, ulysses - 1 + sources - 1)

    def landing(what, h, whose):
        if what == 0:
            return kraw.at[h, pl.ds(whose * local, local), :]
        if what == 1:
            return tab_v.at[h, pl.ds(home + whose * local, local), :]
        return qbuf.at[h, pl.ds(whose * local, local), :]

    def leaving(what, h, whose):
        width = qw if what == 2 else HD
        ref = (k_ref, v_ref, q_ref)[what]
        return ref.at[:, pl.ds(pl.multiple_of((whose * kvl + h) * width, width), width)]

    def incoming(what, h, i):
        return pltpu.make_async_remote_copy(
            src_ref=leaving(what, h, u_peer(i)), dst_ref=landing(what, h, me),
            send_sem=in_send.at[what, h, i - 1], recv_sem=in_recv.at[what, h, i - 1],
            device_id={"ulysses": u_peer(i)}, device_id_type=MESH,
        )

    def own_in(what, h):
        return pltpu.make_async_copy(leaving(what, h, me), landing(what, h, me), in_local.at[what, h])

    order = [(w, h) for h in range(kvl) for w in (0, 1)] + [(2, h) for h in range(kvl)]
    for what, h in order:
        for i in range(1, ulysses):
            incoming(what, h, i).start()
        own_in(what, h).start()

    def arrive(what, h):
        own_in(what, h).wait()
        for i in range(1, ulysses):
            incoming(what, h, i).wait_recv()

    ends = []
    starts = []
    total = jnp.int32(0)
    for r in range(reqs):
        starts.append(total)
        total = total + pages_ref[pack, r] * PAGE
        ends.append(total)

    def first_token(pos):
        first = jnp.zeros_like(pos)
        for r in range(reqs):
            first = jnp.maximum(first, jnp.where(pos >= starts[r], starts[r], 0))
        return first

    pos_rows = blk * rows + lax.broadcasted_iota(jnp.int32, (rows, HD), 0)
    rel = (pos_rows - first_token(pos_rows)).astype(jnp.float32)
    angles = rel * freq_ref[...]
    lanes = lax.broadcasted_iota(jnp.int32, (rows, HD), 1)
    cos_t[...] = jnp.cos(angles)
    sine = jnp.sin(angles)
    sin_t[...] = jnp.where(lanes < HD // 2, -sine, sine)

    def onward(which, h, hop):
        tab = (tab_k, tab_v)[which]
        return pltpu.make_async_remote_copy(
            src_ref=tab.at[h, pl.ds(home, rows), :],
            dst_ref=tab.at[h, pl.ds((back - hop) * rows, rows), :],
            send_sem=x_send.at[which, h, hop - 1], recv_sem=x_recv.at[which, h, hop - 1],
            device_id={"blk": lax.rem(blk + hop, blks)}, device_id_type=MESH,
        )

    for h in range(kvl):
        arrive(0, h)
        tab_k[h, pl.ds(home, rows), :] = turn(kraw[h], cos_t[...], sin_t[...])
        arrive(1, h)
        for hop in range(1, back + 1):
            @pl.when(blk + hop < blks)
            def _():
                onward(0, h, hop).start()
                onward(1, h, hop).start()

    def page_for(owner):
        def step(j, found):
            page = table_ref[pack, blk * slots + j]
            return found + jnp.where(lax.div(page, jnp.int32(slots)) == owner, j, 0)
        return lax.fori_loop(0, slots, step, jnp.int32(0))

    def handed(which, i):
        src, dst = ((out_k, got_k), (out_v, got_v))[which]
        return pltpu.make_async_remote_copy(
            src_ref=src.at[i], dst_ref=dst.at[mine],
            send_sem=c_send.at[which, i - 1], recv_sem=c_recv.at[which, i - 1],
            device_id=s_peer(i)[1], device_id_type=MESH,
        )

    def own_page(which):
        src, dst = ((out_k, got_k), (out_v, got_v))[which]
        return pltpu.make_async_copy(src.at[0], dst.at[mine], c_local.at[which])

    for i in range(sources):
        chosen = page_for(s_peer(i)[0])
        for tab, out in ((tab_k, out_k), (tab_v, out_v)):
            out[i] = pick(chosen, [tab[:, home + j * PAGE:home + (j + 1) * PAGE, :] for j in range(slots)])
    for i in range(1, sources):
        handed(0, i).start()
        handed(1, i).start()
    own_page(0).start()
    own_page(1).start()

    block = min(rows, 128)
    lead = min(-(-reach // block) * block, home)
    span = lead + block
    chunk = span if span <= 512 else block
    factor = QUERY_SCALE / SOFT_CAP

    def attend(h, i):
        at = i * block
        if not isinstance(i, int):
            at = pl.multiple_of(at, block)
        here = pl.ds(at, block)
        cosine, sine_here = cos_t[here, :], sin_t[here, :]
        query = jnp.concatenate(
            [turn(qbuf[h, here, g * HD:(g + 1) * HD], cosine, sine_here) for g in range(group)], axis=0
        )
        pos = blk * rows + at + lax.broadcasted_iota(jnp.int32, (block, 1), 0)
        low = jnp.maximum(first_token(pos), pos - (WINDOW - 1))
        pos = jnp.concatenate([pos] * group, axis=0)
        low = jnp.concatenate([low] * group, axis=0)
        begin = home + at - lead

        def part(c):
            start = begin + c * chunk
            if not isinstance(start, int):
                start = pl.multiple_of(start, block)
            seen = pl.ds(start, chunk)
            scores = lax.dot_general(
                query, tab_k[h, seen, :], (((1,), (1,)), ((), ())), preferred_element_type=jnp.float32
            )
            weights = jnp.exp(SOFT_CAP * jnp.tanh(scores * factor))
            key_pos = (blk - back) * rows + start + lax.broadcasted_iota(jnp.int32, (1, chunk), 1)
            weights = jnp.where((key_pos <= pos) & (key_pos >= low), weights, 0.0)
            total = jnp.sum(weights, axis=1, keepdims=True)
            mixed = jnp.dot(
                weights.astype(jnp.bfloat16), tab_v[h, seen, :], preferred_element_type=jnp.float32
            )
            return mixed, total

        if span == chunk:
            mixed, total = part(0)
        else:
            def step(c, carry):
                mixed, total = part(c)
                return carry[0] + mixed, carry[1] + total
            mixed, total = lax.fori_loop(
                0, span // chunk, step,
                (jnp.zeros((group * block, HD), jnp.float32), jnp.zeros((group * block, 1), jnp.float32)),
            )
        result = (mixed / total).astype(jnp.bfloat16)
        for g in range(group):
            obuf[h, here, g * HD:(g + 1) * HD] = result[g * block:(g + 1) * block]

    def outgoing(h, i):
        return pltpu.make_async_remote_copy(
            src_ref=obuf.at[h, pl.ds(pl.multiple_of(u_peer(i) * local, local), local), :],
            dst_ref=out_ref.at[:, pl.ds(pl.multiple_of((me * kvl + h) * qw, qw), qw)],
            send_sem=o_send.at[h, i - 1], recv_sem=o_recv.at[h, i - 1],
            device_id={"ulysses": u_peer(i)}, device_id_type=MESH,
        )

    def own_out(h):
        return pltpu.make_async_copy(
            obuf.at[h, pl.ds(pl.multiple_of(me * local, local), local), :],
            out_ref.at[:, pl.ds(pl.multiple_of((me * kvl + h) * qw, qw), qw)],
            o_local.at[h],
        )

    for h in range(kvl):
        for hop in range(1, back + 1):
            @pl.when(blk >= hop)
            def _():
                onward(0, h, hop).wait_recv()
                onward(1, h, hop).wait_recv()
        arrive(2, h)
        if rows // block <= 4:
            for i in range(rows // block):
                attend(h, i)
        else:
            def each(i, carry):
                attend(h, i)
                return carry
            lax.fori_loop(0, rows // block, each, 0)
        for i in range(1, ulysses):
            outgoing(h, i).start()
        own_out(h).start()

    own_page(0).wait()
    own_page(1).wait()
    for i in range(1, sources):
        handed(0, i).wait_recv()
        handed(1, i).wait_recv()
    for i in range(1, sources):
        handed(0, i).wait_send()
        handed(1, i).wait_send()
    for what, h in order:
        for i in range(1, ulysses):
            incoming(what, h, i).wait_send()
    for h in range(kvl):
        for hop in range(1, back + 1):
            @pl.when(blk + hop < blks)
            def _():
                onward(0, h, hop).wait_send()
                onward(1, h, hop).wait_send()
    for h in range(kvl):
        own_out(h).wait()
        for i in range(1, ulysses):
            outgoing(h, i).wait()


def place(sizes, table_ref, got_k, got_v, att_ref, out_ref, ck_ref, cv_ref, sem):
    blks, cores, slots = sizes
    sources = blks * cores
    mine = lax.axis_index("blk") * cores + lax.axis_index("handoff")
    copies = [pltpu.make_async_copy(att_ref, out_ref, sem.at[2 * slots])]
    copies[0].start()
    for j in range(slots):
        def step(n, found, j=j):
            s = n // slots
            page = table_ref[lax.rem(s, cores), (s // cores) * slots + lax.rem(n, slots)]
            return found + jnp.where(page == mine * slots + j, s, 0)
        source = lax.fori_loop(0, sources * slots, step, jnp.int32(0))
        for which, (got, cache) in enumerate(((got_k, ck_ref), (got_v, cv_ref))):
            copies.append(pltpu.make_async_copy(got.at[source], cache.at[j], sem.at[2 * j + which]))
            copies[-1].start()
    for copy in copies:
        copy.wait()


def body(queries, keys, values, request_pages, page_table):
    local = queries.shape[1]
    ulysses = lax.axis_size("ulysses")
    blks = lax.axis_size("blk")
    cores = lax.axis_size("handoff")
    kvl = KVH // ulysses
    group = QH // KVH
    rows = local * ulysses
    slots = rows // PAGE
    sources = blks * cores
    assert slots == sources
    reach = min(WINDOW, page_table.shape[1] // 2 * PAGE)
    back = min(-(-reach // rows), blks - 1)
    reqs = request_pages.shape[1]
    half = np.arange(HD // 2, dtype=np.float64)
    freq = (ROPE_BASE ** (-2.0 * half / HD)).astype(np.float32)
    freq = jnp.asarray(np.concatenate([freq, freq])[None, :])
    sizes = (ulysses, blks, cores, local, kvl, group, reach, reqs)
    qw = group * HD
    bf = jnp.bfloat16
    dma = pltpu.SemaphoreType.DMA
    hops = max(back, 1)
    anywhere = pl.BlockSpec(memory_space=pl.ANY)
    vmem = pl.BlockSpec(memory_space=pltpu.VMEM)
    smem = pl.BlockSpec(memory_space=pltpu.SMEM)
    moved, pages_k, pages_v = pl.pallas_call(
        functools.partial(kernel, sizes),
        out_shape=(
            pltpu.VMEM((local, QH * HD), bf),
            pltpu.VMEM((sources, kvl, PAGE, HD), bf),
            pltpu.VMEM((sources, kvl, PAGE, HD), bf),
        ),
        in_specs=[anywhere, anywhere, anywhere, vmem, smem, smem],
        out_specs=(vmem, vmem, vmem),
        scratch_shapes=[
            pltpu.VMEM((kvl, rows, HD), bf),
            pltpu.VMEM((kvl, (back + 1) * rows, HD), bf),
            pltpu.VMEM((kvl, (back + 1) * rows, HD), bf),
            pltpu.VMEM((kvl, rows, qw), bf),
            pltpu.VMEM((kvl, rows, qw), bf),
            pltpu.VMEM((rows, HD), jnp.float32),
            pltpu.VMEM((rows, HD), jnp.float32),
            pltpu.VMEM((sources, kvl, PAGE, HD), bf),
            pltpu.VMEM((sources, kvl, PAGE, HD), bf),
            dma((3, kvl, ulysses - 1)),
            dma((3, kvl, ulysses - 1)),
            dma((3, kvl)),
            dma((2, kvl, hops)),
            dma((2, kvl, hops)),
            dma((2, sources - 1)),
            dma((2, sources - 1)),
            dma((2,)),
            dma((kvl, ulysses - 1)),
            dma((kvl, ulysses - 1)),
            dma((kvl,)),
        ],
        compiler_params=pltpu.CompilerParams(collective_id=0, has_side_effects=True),
    )(queries[0], keys[0], values[0], freq, request_pages, page_table)
    pages_k, pages_v, moved = (
        pltpu.with_memory_space_constraint(x, pltpu.VMEM) for x in (pages_k, pages_v, moved)
    )
    attended, cache_keys, cache_values = pl.pallas_call(
        functools.partial(place, (blks, cores, slots)),
        out_shape=(
            jax.ShapeDtypeStruct((local, QH * HD), bf),
            jax.ShapeDtypeStruct((slots, kvl, PAGE, HD), bf),
            jax.ShapeDtypeStruct((slots, kvl, PAGE, HD), bf),
        ),
        in_specs=[smem, anywhere, anywhere, anywhere],
        out_specs=(anywhere, anywhere, anywhere),
        scratch_shapes=[dma((2 * slots + 1,))],
        compiler_params=pltpu.CompilerParams(vmem_limit_bytes=1 << 20),
    )(page_table, pages_k, pages_v, moved)
    return (attended[None], cache_keys, cache_values)


def solution(mesh):
    in_specs = (
        P(("groups", "handoff"), ("blk", "ulysses"), None),
        P(("groups", "handoff"), ("blk", "ulysses"), None),
        P(("groups", "handoff"), ("blk", "ulysses"), None),
        P("groups", None),
        P("groups", None),
    )
    out_specs = (
        P(("groups", "handoff"), ("blk", "ulysses"), None),
        P(("groups", "blk", "handoff"), "ulysses", None, None),
        P(("groups", "blk", "handoff"), "ulysses", None, None),
    )
    return jax.shard_map(body, mesh=mesh, in_specs=in_specs, out_specs=out_specs, check_vma=False)
```

```python
import functools

import jax
import jax.numpy as jnp
import numpy as np
from jax import lax
from jax.experimental import pallas as pl
from jax.experimental.pallas import tpu as pltpu
from jax.sharding import PartitionSpec as P

QH = 32
KVH = 16
HD = 128
WINDOW = 4096
PAGE = 64

QUERY_SCALE = 144.0 ** (-0.5)
SOFT_CAP = 50.0
ROPE_BASE = 10000.0
MESH = pl.DeviceIdType.MESH


def turn(x, cosine, sine):
    wide = x.astype(jnp.float32)
    return (wide * cosine + pltpu.roll(wide, HD // 2, 1) * sine).astype(jnp.bfloat16)


def pick(index, choices):
    chosen = choices[0]
    for j in range(1, len(choices)):
        chosen = jnp.where(index == j, choices[j], chosen)
    return chosen


def kernel(
    sizes, q_ref, k_ref, v_ref, freq_ref, pages_ref, table_ref,
    out_ref, ck_ref, cv_ref,
    kraw, tab_k, tab_v, qbuf, obuf, cos_t, sin_t, out_k, out_v, got_k, got_v,
    in_send, in_recv, in_local, x_send, x_recv, c_send, c_recv, c_local, o_send, o_recv, o_local,
):
    ulysses, blks, cores, local, kvl, group, reach, reqs = sizes
    rows = ulysses * local
    slots = rows // PAGE
    sources = blks * cores
    back = min(-(-reach // rows), blks - 1)
    home = back * rows
    qw = group * HD
    me = lax.axis_index("ulysses")
    blk = lax.axis_index("blk")
    pack = lax.axis_index("handoff")
    mine = blk * cores + pack

    barrier = pltpu.get_barrier_semaphore()

    def u_peer(i):
        return lax.rem(me + i, ulysses)

    def s_peer(i):
        p = lax.rem(mine + i, sources)
        return p, {"blk": p // cores, "handoff": lax.rem(p, cores)}

    for i in range(1, ulysses):
        pl.semaphore_signal(barrier, inc=1, device_id={"ulysses": u_peer(i)}, device_id_type=MESH)
    for i in range(1, sources):
        pl.semaphore_signal(barrier, inc=1, device_id=s_peer(i)[1], device_id_type=MESH)

    for hop in range(1, back + 1):
        @pl.when(blk < hop)
        def _():
            part = pl.ds((back - hop) * rows, rows)
            tab_k[:, part, :] = jnp.zeros((kvl, rows, HD), jnp.bfloat16)
            tab_v[:, part, :] = jnp.zeros((kvl, rows, HD), jnp.bfloat16)

    pl.semaphore_wait(barrier, ulysses - 1 + sources - 1)

    def landing(what, h, whose):
        if what == 0:
            return kraw.at[h, pl.ds(whose * local, local), :]
        if what == 1:
            return tab_v.at[h, pl.ds(home + whose * local, local), :]
        return qbuf.at[h, pl.ds(whose * local, local), :]

    def leaving(what, h, whose):
        width = qw if what == 2 else HD
        ref = (k_ref, v_ref, q_ref)[what]
        return ref.at[:, pl.ds(pl.multiple_of((whose * kvl + h) * width, width), width)]

    def incoming(what, h, i):
        return pltpu.make_async_remote_copy(
            src_ref=leaving(what, h, u_peer(i)), dst_ref=landing(what, h, me),
            send_sem=in_send.at[what, h, i - 1], recv_sem=in_recv.at[what, h, i - 1],
            device_id={"ulysses": u_peer(i)}, device_id_type=MESH,
        )

    def own_in(what, h):
        return pltpu.make_async_copy(leaving(what, h, me), landing(what, h, me), in_local.at[what, h])

    order = [(w, h) for h in range(kvl) for w in (0, 1)] + [(2, h) for h in range(kvl)]
    for what, h in order:
        for i in range(1, ulysses):
            incoming(what, h, i).start()
        own_in(what, h).start()

    def arrive(what, h):
        own_in(what, h).wait()
        for i in range(1, ulysses):
            incoming(what, h, i).wait_recv()

    ends = []
    starts = []
    total = jnp.int32(0)
    for r in range(reqs):
        starts.append(total)
        total = total + pages_ref[pack, r] * PAGE
        ends.append(total)

    def first_token(pos):
        first = jnp.zeros_like(pos)
        for r in range(reqs):
            first = jnp.maximum(first, jnp.where(pos >= starts[r], starts[r], 0))
        return first

    pos_rows = blk * rows + lax.broadcasted_iota(jnp.int32, (rows, HD), 0)
    rel = (pos_rows - first_token(pos_rows)).astype(jnp.float32)
    angles = rel * freq_ref[...]
    lanes = lax.broadcasted_iota(jnp.int32, (rows, HD), 1)
    cos_t[...] = jnp.cos(angles)
    sine = jnp.sin(angles)
    sin_t[...] = jnp.where(lanes < HD // 2, -sine, sine)

    def onward(which, h, hop):
        tab = (tab_k, tab_v)[which]
        return pltpu.make_async_remote_copy(
            src_ref=tab.at[h, pl.ds(home, rows), :],
            dst_ref=tab.at[h, pl.ds((back - hop) * rows, rows), :],
            send_sem=x_send.at[which, h, hop - 1], recv_sem=x_recv.at[which, h, hop - 1],
            device_id={"blk": lax.rem(blk + hop, blks)}, device_id_type=MESH,
        )

    for h in range(kvl):
        arrive(0, h)
        tab_k[h, pl.ds(home, rows), :] = turn(kraw[h], cos_t[...], sin_t[...])
        arrive(1, h)
        for hop in range(1, back + 1):
            @pl.when(blk + hop < blks)
            def _():
                onward(0, h, hop).start()
                onward(1, h, hop).start()

    def page_for(owner):
        def step(j, found):
            page = table_ref[pack, blk * slots + j]
            return found + jnp.where(lax.div(page, jnp.int32(slots)) == owner, j, 0)
        return lax.fori_loop(0, slots, step, jnp.int32(0))

    def handed(which, i):
        src, dst = ((out_k, got_k), (out_v, got_v))[which]
        return pltpu.make_async_remote_copy(
            src_ref=src.at[i], dst_ref=dst.at[mine],
            send_sem=c_send.at[which, i - 1], recv_sem=c_recv.at[which, i - 1],
            device_id=s_peer(i)[1], device_id_type=MESH,
        )

    def own_page(which):
        src, dst = ((out_k, got_k), (out_v, got_v))[which]
        return pltpu.make_async_copy(src.at[0], dst.at[mine], c_local.at[which])

    for i in range(sources):
        chosen = page_for(s_peer(i)[0])
        for tab, out in ((tab_k, out_k), (tab_v, out_v)):
            out[i] = pick(chosen, [tab[:, home + j * PAGE:home + (j + 1) * PAGE, :] for j in range(slots)])
    for i in range(1, sources):
        handed(0, i).start()
        handed(1, i).start()
    own_page(0).start()
    own_page(1).start()

    block = min(rows, 128)
    lead = min(-(-reach // block) * block, home)
    span = lead + block
    chunk = span if span <= 512 else block
    factor = QUERY_SCALE / SOFT_CAP

    def attend(h, i):
        at = i * block
        if not isinstance(i, int):
            at = pl.multiple_of(at, block)
        here = pl.ds(at, block)
        cosine, sine_here = cos_t[here, :], sin_t[here, :]
        query = jnp.concatenate(
            [turn(qbuf[h, here, g * HD:(g + 1) * HD], cosine, sine_here) for g in range(group)], axis=0
        )
        pos = blk * rows + at + lax.broadcasted_iota(jnp.int32, (block, 1), 0)
        low = jnp.maximum(first_token(pos), pos - (WINDOW - 1))
        pos = jnp.concatenate([pos] * group, axis=0)
        low = jnp.concatenate([low] * group, axis=0)
        begin = home + at - lead

        def part(c):
            start = begin + c * chunk
            if not isinstance(start, int):
                start = pl.multiple_of(start, block)
            seen = pl.ds(start, chunk)
            scores = lax.dot_general(
                query, tab_k[h, seen, :], (((1,), (1,)), ((), ())), preferred_element_type=jnp.float32
            )
            weights = jnp.exp(SOFT_CAP * jnp.tanh(scores * factor))
            key_pos = (blk - back) * rows + start + lax.broadcasted_iota(jnp.int32, (1, chunk), 1)
            weights = jnp.where((key_pos <= pos) & (key_pos >= low), weights, 0.0)
            total = jnp.sum(weights, axis=1, keepdims=True)
            mixed = jnp.dot(
                weights.astype(jnp.bfloat16), tab_v[h, seen, :], preferred_element_type=jnp.float32
            )
            return mixed, total

        if span == chunk:
            mixed, total = part(0)
        else:
            def step(c, carry):
                mixed, total = part(c)
                return carry[0] + mixed, carry[1] + total
            mixed, total = lax.fori_loop(
                0, span // chunk, step,
                (jnp.zeros((group * block, HD), jnp.float32), jnp.zeros((group * block, 1), jnp.float32)),
            )
        result = (mixed / total).astype(jnp.bfloat16)
        for g in range(group):
            obuf[h, here, g * HD:(g + 1) * HD] = result[g * block:(g + 1) * block]

    def outgoing(h, i):
        return pltpu.make_async_remote_copy(
            src_ref=obuf.at[h, pl.ds(pl.multiple_of(u_peer(i) * local, local), local), :],
            dst_ref=out_ref.at[:, pl.ds(pl.multiple_of((me * kvl + h) * qw, qw), qw)],
            send_sem=o_send.at[h, i - 1], recv_sem=o_recv.at[h, i - 1],
            device_id={"ulysses": u_peer(i)}, device_id_type=MESH,
        )

    def own_out(h):
        return pltpu.make_async_copy(
            obuf.at[h, pl.ds(pl.multiple_of(me * local, local), local), :],
            out_ref.at[:, pl.ds(pl.multiple_of((me * kvl + h) * qw, qw), qw)],
            o_local.at[h],
        )

    for h in range(kvl):
        for hop in range(1, back + 1):
            @pl.when(blk >= hop)
            def _():
                onward(0, h, hop).wait_recv()
                onward(1, h, hop).wait_recv()
        arrive(2, h)
        if rows // block <= 4:
            for i in range(rows // block):
                attend(h, i)
        else:
            def each(i, carry):
                attend(h, i)
                return carry
            lax.fori_loop(0, rows // block, each, 0)
        for i in range(1, ulysses):
            outgoing(h, i).start()
        own_out(h).start()

    own_page(0).wait()
    own_page(1).wait()
    for i in range(1, sources):
        handed(0, i).wait_recv()
        handed(1, i).wait_recv()
    for j in range(slots):
        def step(n, found, j=j):
            s = n // slots
            page = table_ref[lax.rem(s, cores), (s // cores) * slots + lax.rem(n, slots)]
            return found + jnp.where(page == mine * slots + j, s, 0)
        source = lax.fori_loop(0, sources * slots, step, jnp.int32(0))
        ck_ref[j] = pick(source, [got_k[s] for s in range(sources)])
        cv_ref[j] = pick(source, [got_v[s] for s in range(sources)])

    for i in range(1, sources):
        handed(0, i).wait_send()
        handed(1, i).wait_send()
    for what, h in order:
        for i in range(1, ulysses):
            incoming(what, h, i).wait_send()
    for h in range(kvl):
        for hop in range(1, back + 1):
            @pl.when(blk + hop < blks)
            def _():
                onward(0, h, hop).wait_send()
                onward(1, h, hop).wait_send()
    for h in range(kvl):
        own_out(h).wait()
        for i in range(1, ulysses):
            outgoing(h, i).wait()


def place(*refs):
    count = (len(refs) - 1) // 2
    sem = refs[-1]
    copies = [pltpu.make_async_copy(refs[i], refs[count + i], sem.at[i]) for i in range(count)]
    for copy in copies:
        copy.start()
    for copy in copies:
        copy.wait()


def body(queries, keys, values, request_pages, page_table):
    local = queries.shape[1]
    ulysses = lax.axis_size("ulysses")
    blks = lax.axis_size("blk")
    cores = lax.axis_size("handoff")
    kvl = KVH // ulysses
    group = QH // KVH
    rows = local * ulysses
    slots = rows // PAGE
    sources = blks * cores
    assert slots == sources
    reach = min(WINDOW, page_table.shape[1] // 2 * PAGE)
    back = min(-(-reach // rows), blks - 1)
    reqs = request_pages.shape[1]
    half = np.arange(HD // 2, dtype=np.float64)
    freq = (ROPE_BASE ** (-2.0 * half / HD)).astype(np.float32)
    freq = jnp.asarray(np.concatenate([freq, freq])[None, :])
    sizes = (ulysses, blks, cores, local, kvl, group, reach, reqs)
    qw = group * HD
    bf = jnp.bfloat16
    dma = pltpu.SemaphoreType.DMA
    hops = max(back, 1)
    anywhere = pl.BlockSpec(memory_space=pl.ANY)
    vmem = pl.BlockSpec(memory_space=pltpu.VMEM)
    smem = pl.BlockSpec(memory_space=pltpu.SMEM)
    results = pl.pallas_call(
        functools.partial(kernel, sizes),
        out_shape=(
            pltpu.VMEM((local, QH * HD), bf),
            pltpu.VMEM((slots, kvl, PAGE, HD), bf),
            pltpu.VMEM((slots, kvl, PAGE, HD), bf),
        ),
        in_specs=[anywhere, anywhere, anywhere, vmem, smem, smem],
        out_specs=(vmem, vmem, vmem),
        scratch_shapes=[
            pltpu.VMEM((kvl, rows, HD), bf),
            pltpu.VMEM((kvl, (back + 1) * rows, HD), bf),
            pltpu.VMEM((kvl, (back + 1) * rows, HD), bf),
            pltpu.VMEM((kvl, rows, qw), bf),
            pltpu.VMEM((kvl, rows, qw), bf),
            pltpu.VMEM((rows, HD), jnp.float32),
            pltpu.VMEM((rows, HD), jnp.float32),
            pltpu.VMEM((sources, kvl, PAGE, HD), bf),
            pltpu.VMEM((sources, kvl, PAGE, HD), bf),
            pltpu.VMEM((sources, kvl, PAGE, HD), bf),
            pltpu.VMEM((sources, kvl, PAGE, HD), bf),
            dma((3, kvl, ulysses - 1)),
            dma((3, kvl, ulysses - 1)),
            dma((3, kvl)),
            dma((2, kvl, hops)),
            dma((2, kvl, hops)),
            dma((2, sources - 1)),
            dma((2, sources - 1)),
            dma((2,)),
            dma((kvl, ulysses - 1)),
            dma((kvl, ulysses - 1)),
            dma((kvl,)),
        ],
        compiler_params=pltpu.CompilerParams(collective_id=0, has_side_effects=True),
    )(queries[0], keys[0], values[0], freq, request_pages, page_table)
    results = [pltpu.with_memory_space_constraint(x, pltpu.VMEM) for x in results]
    attended, cache_keys, cache_values = pl.pallas_call(
        place,
        out_shape=tuple(jax.ShapeDtypeStruct(x.shape, x.dtype) for x in results),
        in_specs=[anywhere] * len(results),
        out_specs=(anywhere,) * len(results),
        scratch_shapes=[dma((len(results),))],
        compiler_params=pltpu.CompilerParams(vmem_limit_bytes=1 << 20),
    )(*results)
    return (attended[None], cache_keys, cache_values)


def solution(mesh):
    in_specs = (
        P(("groups", "handoff"), ("blk", "ulysses"), None),
        P(("groups", "handoff"), ("blk", "ulysses"), None),
        P(("groups", "handoff"), ("blk", "ulysses"), None),
        P("groups", None),
        P("groups", None),
    )
    out_specs = (
        P(("groups", "handoff"), ("blk", "ulysses"), None),
        P(("groups", "blk", "handoff"), "ulysses", None, None),
        P(("groups", "blk", "handoff"), "ulysses", None, None),
    )
    return jax.shard_map(body, mesh=mesh, in_specs=in_specs, out_specs=out_specs, check_vma=False)
```

```python
import functools

import jax
import jax.numpy as jnp
import numpy as np
from jax import lax
from jax.experimental import pallas as pl
from jax.experimental.pallas import tpu as pltpu
from jax.sharding import PartitionSpec as P

QH = 32
KVH = 16
HD = 128
WINDOW = 4096
PAGE = 64

QUERY_SCALE = 144.0 ** (-0.5)
SOFT_CAP = 50.0
ROPE_BASE = 10000.0
MESH = pl.DeviceIdType.MESH


def turn(x, cosine, sine):
    wide = x.astype(jnp.float32)
    return (wide * cosine + pltpu.roll(wide, HD // 2, 1) * sine).astype(jnp.bfloat16)


def pick(index, choices):
    chosen = choices[0]
    for j in range(1, len(choices)):
        chosen = jnp.where(index == j, choices[j], chosen)
    return chosen


def kernel(
    sizes, q_ref, k_ref, v_ref, freq_ref, pages_ref, table_ref,
    out_ref, ck_ref, cv_ref,
    kraw, tab_k, tab_v, qbuf, obuf, cos_t, sin_t, out_k, out_v, got_k, got_v,
    in_send, in_recv, in_local, x_send, x_recv, c_send, c_recv, c_local, o_send, o_recv, o_local,
):
    ulysses, blks, cores, local, kvl, group, reach, reqs = sizes
    rows = ulysses * local
    slots = rows // PAGE
    sources = blks * cores
    back = min(-(-reach // rows), blks - 1)
    home = back * rows
    qw = group * HD
    me = lax.axis_index("ulysses")
    blk = lax.axis_index("blk")
    pack = lax.axis_index("handoff")
    mine = blk * cores + pack

    barrier = pltpu.get_barrier_semaphore()

    def u_peer(i):
        return lax.rem(me + i, ulysses)

    def s_peer(i):
        p = lax.rem(mine + i, sources)
        return p, {"blk": p // cores, "handoff": lax.rem(p, cores)}

    for i in range(1, ulysses):
        pl.semaphore_signal(barrier, inc=1, device_id={"ulysses": u_peer(i)}, device_id_type=MESH)
    for i in range(1, sources):
        pl.semaphore_signal(barrier, inc=1, device_id=s_peer(i)[1], device_id_type=MESH)

    for hop in range(1, back + 1):
        @pl.when(blk < hop)
        def _():
            part = pl.ds((back - hop) * rows, rows)
            tab_k[:, part, :] = jnp.zeros((kvl, rows, HD), jnp.bfloat16)
            tab_v[:, part, :] = jnp.zeros((kvl, rows, HD), jnp.bfloat16)

    pl.semaphore_wait(barrier, ulysses - 1 + sources - 1)

    def landing(what, h, whose):
        if what == 0:
            return kraw.at[h, pl.ds(whose * local, local), :]
        if what == 1:
            return tab_v.at[h, pl.ds(home + whose * local, local), :]
        return qbuf.at[h, pl.ds(whose * local, local), :]

    def leaving(what, h, whose):
        width = qw if what == 2 else HD
        ref = (k_ref, v_ref, q_ref)[what]
        return ref.at[:, pl.ds(pl.multiple_of((whose * kvl + h) * width, width), width)]

    def incoming(what, h, i):
        return pltpu.make_async_remote_copy(
            src_ref=leaving(what, h, u_peer(i)), dst_ref=landing(what, h, me),
            send_sem=in_send.at[what, h, i - 1], recv_sem=in_recv.at[what, h, i - 1],
            device_id={"ulysses": u_peer(i)}, device_id_type=MESH,
        )

    def own_in(what, h):
        return pltpu.make_async_copy(leaving(what, h, me), landing(what, h, me), in_local.at[what, h])

    order = [(w, h) for h in range(kvl) for w in (0, 1)] + [(2, h) for h in range(kvl)]
    for what, h in order:
        for i in range(1, ulysses):
            incoming(what, h, i).start()
        own_in(what, h).start()

    def arrive(what, h):
        own_in(what, h).wait()
        for i in range(1, ulysses):
            incoming(what, h, i).wait_recv()

    ends = []
    starts = []
    total = jnp.int32(0)
    for r in range(reqs):
        starts.append(total)
        total = total + pages_ref[pack, r] * PAGE
        ends.append(total)

    def first_token(pos):
        first = jnp.zeros_like(pos)
        for r in range(reqs):
            first = jnp.maximum(first, jnp.where(pos >= starts[r], starts[r], 0))
        return first

    pos_rows = blk * rows + lax.broadcasted_iota(jnp.int32, (rows, HD), 0)
    rel = (pos_rows - first_token(pos_rows)).astype(jnp.float32)
    angles = rel * freq_ref[...]
    lanes = lax.broadcasted_iota(jnp.int32, (rows, HD), 1)
    cos_t[...] = jnp.cos(angles)
    sine = jnp.sin(angles)
    sin_t[...] = jnp.where(lanes < HD // 2, -sine, sine)

    def onward(which, h, hop):
        tab = (tab_k, tab_v)[which]
        return pltpu.make_async_remote_copy(
            src_ref=tab.at[h, pl.ds(home, rows), :],
            dst_ref=tab.at[h, pl.ds((back - hop) * rows, rows), :],
            send_sem=x_send.at[which, h, hop - 1], recv_sem=x_recv.at[which, h, hop - 1],
            device_id={"blk": lax.rem(blk + hop, blks)}, device_id_type=MESH,
        )

    for h in range(kvl):
        arrive(0, h)
        tab_k[h, pl.ds(home, rows), :] = turn(kraw[h], cos_t[...], sin_t[...])
        arrive(1, h)
        for hop in range(1, back + 1):
            @pl.when(blk + hop < blks)
            def _():
                onward(0, h, hop).start()
                onward(1, h, hop).start()

    def page_for(owner):
        def step(j, found):
            page = table_ref[pack, blk * slots + j]
            return found + jnp.where(lax.div(page, jnp.int32(slots)) == owner, j, 0)
        return lax.fori_loop(0, slots, step, jnp.int32(0))

    def handed(which, i):
        src, dst = ((out_k, got_k), (out_v, got_v))[which]
        return pltpu.make_async_remote_copy(
            src_ref=src.at[i], dst_ref=dst.at[mine],
            send_sem=c_send.at[which, i - 1], recv_sem=c_recv.at[which, i - 1],
            device_id=s_peer(i)[1], device_id_type=MESH,
        )

    def own_page(which):
        src, dst = ((out_k, got_k), (out_v, got_v))[which]
        return pltpu.make_async_copy(src.at[0], dst.at[mine], c_local.at[which])

    for i in range(sources):
        chosen = page_for(s_peer(i)[0])
        for tab, out in ((tab_k, out_k), (tab_v, out_v)):
            out[i] = pick(chosen, [tab[:, home + j * PAGE:home + (j + 1) * PAGE, :] for j in range(slots)])
    for i in range(1, sources):
        handed(0, i).start()
        handed(1, i).start()
    own_page(0).start()
    own_page(1).start()

    block = min(rows, 128)
    lead = min(-(-reach // block) * block, home)
    span = lead + block
    chunk = span if span <= 512 else block
    factor = QUERY_SCALE / SOFT_CAP

    def attend(h, i):
        at = i * block
        if not isinstance(i, int):
            at = pl.multiple_of(at, block)
        here = pl.ds(at, block)
        cosine, sine_here = cos_t[here, :], sin_t[here, :]
        query = jnp.concatenate(
            [turn(qbuf[h, here, g * HD:(g + 1) * HD], cosine, sine_here) for g in range(group)], axis=0
        )
        pos = blk * rows + at + lax.broadcasted_iota(jnp.int32, (block, 1), 0)
        low = jnp.maximum(first_token(pos), pos - (WINDOW - 1))
        pos = jnp.concatenate([pos] * group, axis=0)
        low = jnp.concatenate([low] * group, axis=0)
        begin = home + at - lead

        def part(c):
            start = begin + c * chunk
            if not isinstance(start, int):
                start = pl.multiple_of(start, block)
            seen = pl.ds(start, chunk)
            scores = lax.dot_general(
                query, tab_k[h, seen, :], (((1,), (1,)), ((), ())), preferred_element_type=jnp.float32
            )
            weights = jnp.exp(SOFT_CAP * jnp.tanh(scores * factor))
            key_pos = (blk - back) * rows + start + lax.broadcasted_iota(jnp.int32, (1, chunk), 1)
            weights = jnp.where((key_pos <= pos) & (key_pos >= low), weights, 0.0)
            total = jnp.sum(weights, axis=1, keepdims=True)
            mixed = jnp.dot(
                weights.astype(jnp.bfloat16), tab_v[h, seen, :], preferred_element_type=jnp.float32
            )
            return mixed, total

        if span == chunk:
            mixed, total = part(0)
        else:
            def step(c, carry):
                mixed, total = part(c)
                return carry[0] + mixed, carry[1] + total
            mixed, total = lax.fori_loop(
                0, span // chunk, step,
                (jnp.zeros((group * block, HD), jnp.float32), jnp.zeros((group * block, 1), jnp.float32)),
            )
        result = (mixed / total).astype(jnp.bfloat16)
        for g in range(group):
            obuf[h, here, g * HD:(g + 1) * HD] = result[g * block:(g + 1) * block]

    def outgoing(h, i):
        return pltpu.make_async_remote_copy(
            src_ref=obuf.at[h, pl.ds(pl.multiple_of(u_peer(i) * local, local), local), :],
            dst_ref=out_ref.at[:, pl.ds(pl.multiple_of((me * kvl + h) * qw, qw), qw)],
            send_sem=o_send.at[h, i - 1], recv_sem=o_recv.at[h, i - 1],
            device_id={"ulysses": u_peer(i)}, device_id_type=MESH,
        )

    def own_out(h):
        return pltpu.make_async_copy(
            obuf.at[h, pl.ds(pl.multiple_of(me * local, local), local), :],
            out_ref.at[:, pl.ds(pl.multiple_of((me * kvl + h) * qw, qw), qw)],
            o_local.at[h],
        )

    for h in range(kvl):
        for hop in range(1, back + 1):
            @pl.when(blk >= hop)
            def _():
                onward(0, h, hop).wait_recv()
                onward(1, h, hop).wait_recv()
        arrive(2, h)
        if rows // block <= 4:
            for i in range(rows // block):
                attend(h, i)
        else:
            def each(i, carry):
                attend(h, i)
                return carry
            lax.fori_loop(0, rows // block, each, 0)
        for i in range(1, ulysses):
            outgoing(h, i).start()
        own_out(h).start()

    own_page(0).wait()
    own_page(1).wait()
    for i in range(1, sources):
        handed(0, i).wait_recv()
        handed(1, i).wait_recv()
    for j in range(slots):
        def step(n, found, j=j):
            s = n // slots
            page = table_ref[lax.rem(s, cores), (s // cores) * slots + lax.rem(n, slots)]
            return found + jnp.where(page == mine * slots + j, s, 0)
        source = lax.fori_loop(0, sources * slots, step, jnp.int32(0))
        ck_ref[j] = pick(source, [got_k[s] for s in range(sources)])
        cv_ref[j] = pick(source, [got_v[s] for s in range(sources)])

    for i in range(1, sources):
        handed(0, i).wait_send()
        handed(1, i).wait_send()
    for what, h in order:
        for i in range(1, ulysses):
            incoming(what, h, i).wait_send()
    for h in range(kvl):
        for hop in range(1, back + 1):
            @pl.when(blk + hop < blks)
            def _():
                onward(0, h, hop).wait_send()
                onward(1, h, hop).wait_send()
    for h in range(kvl):
        own_out(h).wait()
        for i in range(1, ulysses):
            outgoing(h, i).wait()


def near_kernel(
    sizes, q_ref, k_ref, v_ref, freq_ref, pages_ref, table_ref,
    out_ref, ck_ref, cv_ref,
    kraw, tab_k, tab_v, qbuf, obuf, cos_t, sin_t, out_k, out_v, got_k, got_v,
    in_send, in_recv, in_local, x_send, x_recv, c_send, c_recv, c_local, o_send, o_recv, o_local,
):
    ulysses, blks, cores, local, kvl, group, reach, reqs = sizes
    rows = ulysses * local
    slots = rows // PAGE
    sources = blks * cores
    back = min(-(-reach // rows), blks - 1)
    home = back * rows
    half = ulysses // 2
    part = half * local
    qw = group * HD
    me = lax.axis_index("ulysses")
    blk = lax.axis_index("blk")
    pack = lax.axis_index("handoff")
    mine = blk * cores + pack
    side = me // half
    member = lax.rem(me, half)
    diagonal = back > 0

    def quarter(a, device):
        return device if a == 0 else lax.rem(device + half, ulysses)

    def h_peer(i):
        return side * half + lax.rem(member + i, half)

    barrier = pltpu.get_barrier_semaphore()

    def u_peer(i):
        return lax.rem(me + i, ulysses)

    def s_peer(i):
        p = lax.rem(mine + i, sources)
        return p, {"blk": p // cores, "handoff": lax.rem(p, cores)}

    for i in range(1, ulysses):
        pl.semaphore_signal(barrier, inc=1, device_id={"ulysses": u_peer(i)}, device_id_type=MESH)
    for i in range(1, sources):
        pl.semaphore_signal(barrier, inc=1, device_id=s_peer(i)[1], device_id_type=MESH)

    if diagonal:
        @pl.when((side == 0) & (blk > 0))
        def _():
            pl.semaphore_signal(
                barrier, inc=1, device_id={"blk": lax.rem(blk + blks - 1, blks), "ulysses": quarter(1, me)},
                device_id_type=MESH,
            )

    for hop in range(1, back + 1):
        @pl.when(blk < hop)
        def _():
            gap = pl.ds((back - hop) * rows, rows)
            tab_k[:, :, gap, :] = jnp.zeros((2, kvl, rows, HD), jnp.bfloat16)
            tab_v[:, :, gap, :] = jnp.zeros((2, kvl, rows, HD), jnp.bfloat16)

    greeted = ulysses - 1 + sources - 1
    if diagonal:
        awaited = (side == 1) & (blk + 1 < blks)

        @pl.when(awaited)
        def _():
            pl.semaphore_wait(barrier, greeted + 1)

        @pl.when(jnp.logical_not(awaited))
        def _():
            pl.semaphore_wait(barrier, greeted)
    else:
        pl.semaphore_wait(barrier, greeted)

    def landing(what, a, h, whose):
        if what == 0:
            return kraw.at[a, h, pl.ds(whose * local, local), :]
        if what == 1:
            return tab_v.at[a, h, pl.ds(home + whose * local, local), :]
        return qbuf.at[a, h, pl.ds(lax.rem(whose, half) * local, local), :]

    def leaving(what, a, h, whose):
        width = qw if what == 2 else HD
        ref = (k_ref, v_ref, q_ref)[what]
        return ref.at[:, pl.ds(pl.multiple_of((quarter(a, whose) * kvl + h) * width, width), width)]

    def incoming(what, a, h, i):
        peer = h_peer(i) if what == 2 else u_peer(i)
        return pltpu.make_async_remote_copy(
            src_ref=leaving(what, a, h, peer), dst_ref=landing(what, a, h, me),
            send_sem=in_send.at[what, a, h, i - 1], recv_sem=in_recv.at[what, a, h, i - 1],
            device_id={"ulysses": peer}, device_id_type=MESH,
        )

    def own_in(what, a, h):
        return pltpu.make_async_copy(
            leaving(what, a, h, me), landing(what, a, h, me), in_local.at[what, a, h]
        )

    def each_send(what, a, act):
        for i in range(1, half if what == 2 else ulysses):
            if what == 2 or a == 0:
                act(i)
            else:
                @pl.when(u_peer(i) // half >= side)
                def _(i=i):
                    act(i)

    def each_receive(what, a, act):
        for i in range(1, half if what == 2 else ulysses):
            if what == 2 or a == 0:
                act(i)
            else:
                @pl.when(lax.rem(me + ulysses - i, ulysses) // half <= side)
                def _(i=i):
                    act(i)

    order = [(w, a, h) for a in (0, 1) for h in range(kvl) for w in (0, 1)]
    order += [(2, a, h) for a in (0, 1) for h in range(kvl)]
    for what, a, h in order:
        each_send(what, a, lambda i, what=what, a=a, h=h: incoming(what, a, h, i).start())
        own_in(what, a, h).start()

    def arrive(what, a, h):
        own_in(what, a, h).wait()
        each_receive(what, a, lambda i: incoming(what, a, h, i).wait_recv())

    ends = []
    starts = []
    total = jnp.int32(0)
    for r in range(reqs):
        starts.append(total)
        total = total + pages_ref[pack, r] * PAGE
        ends.append(total)

    def first_token(pos):
        first = jnp.zeros_like(pos)
        for r in range(reqs):
            first = jnp.maximum(first, jnp.where(pos >= starts[r], starts[r], 0))
        return first

    pos_rows = blk * rows + lax.broadcasted_iota(jnp.int32, (rows, HD), 0)
    rel = (pos_rows - first_token(pos_rows)).astype(jnp.float32)
    angles = rel * freq_ref[...]
    lanes = lax.broadcasted_iota(jnp.int32, (rows, HD), 1)
    cos_t[...] = jnp.cos(angles)
    sine = jnp.sin(angles)
    sin_t[...] = jnp.where(lanes < HD // 2, -sine, sine)

    def onward(kind, which, h):
        tab = (tab_k, tab_v)[which]
        begin, length = (0, rows) if kind == 0 else (side * part, part)
        source = 1 if kind == 1 else 0
        target = 0 if kind == 0 else 1
        device = {"blk": lax.rem(blk + 1, blks)}
        if kind == 2:
            device["ulysses"] = quarter(1, me)
            begin = part
        return pltpu.make_async_remote_copy(
            src_ref=tab.at[source, h, pl.ds(home + begin, length), :],
            dst_ref=tab.at[target, h, pl.ds(begin, length), :],
            send_sem=x_send.at[kind, which, h], recv_sem=x_recv.at[kind, which, h],
            device_id=device, device_id_type=MESH,
        )

    for a in (0, 1):
        for h in range(kvl):
            arrive(0, a, h)
            first = rows if a == 0 else part
            tab_k[a, h, pl.ds(home, first), :] = turn(
                kraw[a, h, pl.ds(0, first), :], cos_t[pl.ds(0, first), :], sin_t[pl.ds(0, first), :]
            )
            if a == 1:
                @pl.when(side == 1)
                def _(h=h):
                    rest = pl.ds(part, part)
                    tab_k[1, h, pl.ds(home + part, part), :] = turn(
                        kraw[1, h, rest, :], cos_t[rest, :], sin_t[rest, :]
                    )
            arrive(1, a, h)
            if diagonal:
                @pl.when(blk + 1 < blks)
                def _(a=a, h=h):
                    onward(a, 0, h).start()
                    onward(a, 1, h).start()
                if a == 0:
                    @pl.when((blk + 1 < blks) & (side == 1))
                    def _(h=h):
                        onward(2, 0, h).start()
                        onward(2, 1, h).start()

    def page_for(owner):
        def step(j, found):
            page = table_ref[pack, blk * slots + j]
            return found + jnp.where(lax.div(page, jnp.int32(slots)) == owner, j, 0)
        return lax.fori_loop(0, slots, step, jnp.int32(0))

    def handed(which, i):
        src, dst = ((out_k, got_k), (out_v, got_v))[which]
        return pltpu.make_async_remote_copy(
            src_ref=src.at[i], dst_ref=dst.at[mine],
            send_sem=c_send.at[which, i - 1], recv_sem=c_recv.at[which, i - 1],
            device_id=s_peer(i)[1], device_id_type=MESH,
        )

    def own_page(which):
        src, dst = ((out_k, got_k), (out_v, got_v))[which]
        return pltpu.make_async_copy(src.at[0], dst.at[mine], c_local.at[which])

    for i in range(sources):
        chosen = page_for(s_peer(i)[0])
        for tab, out in ((tab_k, out_k), (tab_v, out_v)):
            out[i] = pick(chosen, [tab[0, :, home + j * PAGE:home + (j + 1) * PAGE, :] for j in range(slots)])
    for i in range(1, sources):
        handed(0, i).start()
        handed(1, i).start()
    own_page(0).start()
    own_page(1).start()

    block = part
    lead = min(-(-reach // block) * block, home)
    span = lead + block
    chunk = span
    factor = QUERY_SCALE / SOFT_CAP

    def attend(a, h, at):
        here = pl.ds(at, block)
        cosine, sine_here = cos_t[here, :], sin_t[here, :]
        query = jnp.concatenate(
            [turn(qbuf[a, h, :, g * HD:(g + 1) * HD], cosine, sine_here) for g in range(group)], axis=0
        )
        pos = blk * rows + at + lax.broadcasted_iota(jnp.int32, (block, 1), 0)
        low = jnp.maximum(first_token(pos), pos - (WINDOW - 1))
        pos = jnp.concatenate([pos] * group, axis=0)
        low = jnp.concatenate([low] * group, axis=0)
        begin = home + at - lead

        def piece():
            start = begin
            seen = pl.ds(start, chunk)
            scores = lax.dot_general(
                query, tab_k[a, h, seen, :], (((1,), (1,)), ((), ())), preferred_element_type=jnp.float32
            )
            weights = jnp.exp(SOFT_CAP * jnp.tanh(scores * factor))
            key_pos = (blk - back) * rows + start + lax.broadcasted_iota(jnp.int32, (1, chunk), 1)
            weights = jnp.where((key_pos <= pos) & (key_pos >= low), weights, 0.0)
            total = jnp.sum(weights, axis=1, keepdims=True)
            mixed = jnp.dot(
                weights.astype(jnp.bfloat16), tab_v[a, h, seen, :], preferred_element_type=jnp.float32
            )
            return mixed, total

        mixed, total = piece()
        result = (mixed / total).astype(jnp.bfloat16)
        for g in range(group):
            obuf[a, h, :, g * HD:(g + 1) * HD] = result[g * block:(g + 1) * block]

    def columns(a, h):
        return out_ref.at[:, pl.ds(pl.multiple_of((quarter(a, me) * kvl + h) * qw, qw), qw)]

    def finished(a, h, device):
        start = pl.multiple_of(lax.rem(device, half) * local, local)
        return obuf.at[a, h, pl.ds(start, local), :]

    def outgoing(a, h, i):
        return pltpu.make_async_remote_copy(
            src_ref=finished(a, h, h_peer(i)), dst_ref=columns(a, h),
            send_sem=o_send.at[a, h, i - 1], recv_sem=o_recv.at[a, h, i - 1],
            device_id={"ulysses": h_peer(i)}, device_id_type=MESH,
        )

    def own_out(a, h):
        return pltpu.make_async_copy(finished(a, h, me), columns(a, h), o_local.at[a, h])

    for a in (0, 1):
        for h in range(kvl):
            if diagonal:
                @pl.when(blk > 0)
                def _(a=a, h=h):
                    onward(a, 0, h).wait_recv()
                    onward(a, 1, h).wait_recv()
                if a == 1:
                    @pl.when((blk > 0) & (side == 0))
                    def _(h=h):
                        onward(2, 0, h).wait_recv()
                        onward(2, 1, h).wait_recv()
            arrive(2, a, h)
            for where in (0, 1):
                @pl.when(side == where)
                def _(a=a, h=h, where=where):
                    attend(a, h, where * part)
            for i in range(1, half):
                outgoing(a, h, i).start()
            own_out(a, h).start()

    own_page(0).wait()
    own_page(1).wait()
    for i in range(1, sources):
        handed(0, i).wait_recv()
        handed(1, i).wait_recv()
    for j in range(slots):
        def step(n, found, j=j):
            s = n // slots
            page = table_ref[lax.rem(s, cores), (s // cores) * slots + lax.rem(n, slots)]
            return found + jnp.where(page == mine * slots + j, s, 0)
        source = lax.fori_loop(0, sources * slots, step, jnp.int32(0))
        ck_ref[j] = pick(source, [got_k[s] for s in range(sources)])
        cv_ref[j] = pick(source, [got_v[s] for s in range(sources)])

    for i in range(1, sources):
        handed(0, i).wait_send()
        handed(1, i).wait_send()
    for what, a, h in order:
        each_send(what, a, lambda i, what=what, a=a, h=h: incoming(what, a, h, i).wait_send())
    for h in range(kvl):
        if diagonal:
            @pl.when(blk + 1 < blks)
            def _(h=h):
                for kind in (0, 1):
                    onward(kind, 0, h).wait_send()
                    onward(kind, 1, h).wait_send()

            @pl.when((blk + 1 < blks) & (side == 1))
            def _(h=h):
                onward(2, 0, h).wait_send()
                onward(2, 1, h).wait_send()
    for a in (0, 1):
        for h in range(kvl):
            own_out(a, h).wait()
            for i in range(1, half):
                outgoing(a, h, i).wait()


def place(*refs):
    count = (len(refs) - 1) // 2
    sem = refs[-1]
    copies = [pltpu.make_async_copy(refs[i], refs[count + i], sem.at[i]) for i in range(count)]
    for copy in copies:
        copy.start()
    for copy in copies:
        copy.wait()


def body(queries, keys, values, request_pages, page_table):
    local = queries.shape[1]
    ulysses = lax.axis_size("ulysses")
    blks = lax.axis_size("blk")
    cores = lax.axis_size("handoff")
    kvl = KVH // ulysses
    group = QH // KVH
    rows = local * ulysses
    slots = rows // PAGE
    sources = blks * cores
    assert slots == sources
    reach = min(WINDOW, page_table.shape[1] // 2 * PAGE)
    back = min(-(-reach // rows), blks - 1)
    reqs = request_pages.shape[1]
    half = np.arange(HD // 2, dtype=np.float64)
    freq = (ROPE_BASE ** (-2.0 * half / HD)).astype(np.float32)
    freq = jnp.asarray(np.concatenate([freq, freq])[None, :])
    sizes = (ulysses, blks, cores, local, kvl, group, reach, reqs)
    qw = group * HD
    bf = jnp.bfloat16
    dma = pltpu.SemaphoreType.DMA
    hops = max(back, 1)
    near = reach <= rows and ulysses % 2 == 0 and ulysses > 2
    sets = (2,) if near else ()
    mates = (ulysses // 2 if near else ulysses) - 1
    asked = mates + 1 if near else ulysses
    anywhere = pl.BlockSpec(memory_space=pl.ANY)
    vmem = pl.BlockSpec(memory_space=pltpu.VMEM)
    smem = pl.BlockSpec(memory_space=pltpu.SMEM)
    results = pl.pallas_call(
        functools.partial(near_kernel if near else kernel, sizes),
        out_shape=(
            pltpu.VMEM((local, QH * HD), bf),
            pltpu.VMEM((slots, kvl, PAGE, HD), bf),
            pltpu.VMEM((slots, kvl, PAGE, HD), bf),
        ),
        in_specs=[anywhere, anywhere, anywhere, vmem, smem, smem],
        out_specs=(vmem, vmem, vmem),
        scratch_shapes=[
            pltpu.VMEM(sets + (kvl, rows, HD), bf),
            pltpu.VMEM(sets + (kvl, (back + 1) * rows, HD), bf),
            pltpu.VMEM(sets + (kvl, (back + 1) * rows, HD), bf),
            pltpu.VMEM(sets + (kvl, asked * local, qw), bf),
            pltpu.VMEM(sets + (kvl, asked * local, qw), bf),
            pltpu.VMEM((rows, HD), jnp.float32),
            pltpu.VMEM((rows, HD), jnp.float32),
            pltpu.VMEM((sources, kvl, PAGE, HD), bf),
            pltpu.VMEM((sources, kvl, PAGE, HD), bf),
            pltpu.VMEM((sources, kvl, PAGE, HD), bf),
            pltpu.VMEM((sources, kvl, PAGE, HD), bf),
            dma((3,) + sets + (kvl, ulysses - 1)),
            dma((3,) + sets + (kvl, ulysses - 1)),
            dma((3,) + sets + (kvl,)),
            dma((3, 2, kvl) if near else (2, kvl, hops)),
            dma((3, 2, kvl) if near else (2, kvl, hops)),
            dma((2, sources - 1)),
            dma((2, sources - 1)),
            dma((2,)),
            dma(sets + (kvl, mates)),
            dma(sets + (kvl, mates)),
            dma(sets + (kvl,)),
        ],
        compiler_params=pltpu.CompilerParams(collective_id=1 if near else 0, has_side_effects=True),
    )(queries[0], keys[0], values[0], freq, request_pages, page_table)
    results = [pltpu.with_memory_space_constraint(x, pltpu.VMEM) for x in results]
    attended, cache_keys, cache_values = pl.pallas_call(
        place,
        out_shape=tuple(jax.ShapeDtypeStruct(x.shape, x.dtype) for x in results),
        in_specs=[anywhere] * len(results),
        out_specs=(anywhere,) * len(results),
        scratch_shapes=[dma((len(results),))],
        compiler_params=pltpu.CompilerParams(vmem_limit_bytes=1 << 20),
    )(*results)
    return (attended[None], cache_keys, cache_values)


def solution(mesh):
    in_specs = (
        P(("groups", "handoff"), ("blk", "ulysses"), None),
        P(("groups", "handoff"), ("blk", "ulysses"), None),
        P(("groups", "handoff"), ("blk", "ulysses"), None),
        P("groups", None),
        P("groups", None),
    )
    out_specs = (
        P(("groups", "handoff"), ("blk", "ulysses"), None),
        P(("groups", "blk", "handoff"), "ulysses", None, None),
        P(("groups", "blk", "handoff"), "ulysses", None, None),
    )
    return jax.shard_map(body, mesh=mesh, in_specs=in_specs, out_specs=out_specs, check_vma=False)
```

```python
import functools

import jax
import jax.numpy as jnp
import numpy as np
from jax import lax
from jax.experimental import pallas as pl
from jax.experimental.pallas import tpu as pltpu
from jax.sharding import PartitionSpec as P

QH = 32
KVH = 16
HD = 128
WINDOW = 4096
PAGE = 64

QUERY_SCALE = 144.0 ** (-0.5)
SOFT_CAP = 50.0
ROPE_BASE = 10000.0
MESH = pl.DeviceIdType.MESH


def turn(x, cosine, sine):
    wide = x.astype(jnp.float32)
    return (wide * cosine + pltpu.roll(wide, HD // 2, 1) * sine).astype(jnp.bfloat16)


def pick(index, choices):
    chosen = choices[0]
    for j in range(1, len(choices)):
        chosen = jnp.where(index == j, choices[j], chosen)
    return chosen


def kernel(
    sizes, q_ref, k_ref, v_ref, freq_ref, pages_ref, table_ref,
    out_ref, ck_ref, cv_ref,
    kraw, tab_k, tab_v, qbuf, obuf, cos_t, sin_t, out_k, out_v, got_k, got_v,
    in_send, in_recv, in_local, x_send, x_recv, c_send, c_recv, c_local, o_send, o_recv, o_local,
):
    ulysses, blks, cores, local, kvl, group, reach, reqs = sizes
    rows = ulysses * local
    slots = rows // PAGE
    sources = blks * cores
    back = min(-(-reach // rows), blks - 1)
    home = back * rows
    qw = group * HD
    me = lax.axis_index("ulysses")
    blk = lax.axis_index("blk")
    pack = lax.axis_index("handoff")
    mine = blk * cores + pack

    barrier = pltpu.get_barrier_semaphore()

    def u_peer(i):
        return lax.rem(me + i, ulysses)

    def s_peer(i):
        p = lax.rem(mine + i, sources)
        return p, {"blk": p // cores, "handoff": lax.rem(p, cores)}

    for i in range(1, ulysses):
        pl.semaphore_signal(barrier, inc=1, device_id={"ulysses": u_peer(i)}, device_id_type=MESH)
    for i in range(1, sources):
        pl.semaphore_signal(barrier, inc=1, device_id=s_peer(i)[1], device_id_type=MESH)

    for hop in range(1, back + 1):
        @pl.when(blk < hop)
        def _():
            part = pl.ds((back - hop) * rows, rows)
            tab_k[:, part, :] = jnp.zeros((kvl, rows, HD), jnp.bfloat16)
            tab_v[:, part, :] = jnp.zeros((kvl, rows, HD), jnp.bfloat16)

    pl.semaphore_wait(barrier, ulysses - 1 + sources - 1)

    def landing(what, h, whose):
        if what == 0:
            return kraw.at[h, pl.ds(whose * local, local), :]
        if what == 1:
            return tab_v.at[h, pl.ds(home + whose * local, local), :]
        return qbuf.at[h, pl.ds(whose * local, local), :]

    def leaving(what, h, whose):
        width = qw if what == 2 else HD
        ref = (k_ref, v_ref, q_ref)[what]
        return ref.at[:, pl.ds(pl.multiple_of((whose * kvl + h) * width, width), width)]

    def incoming(what, h, i):
        return pltpu.make_async_remote_copy(
            src_ref=leaving(what, h, u_peer(i)), dst_ref=landing(what, h, me),
            send_sem=in_send.at[what, h, i - 1], recv_sem=in_recv.at[what, h, i - 1],
            device_id={"ulysses": u_peer(i)}, device_id_type=MESH,
        )

    def own_in(what, h):
        return pltpu.make_async_copy(leaving(what, h, me), landing(what, h, me), in_local.at[what, h])

    order = [(w, h) for h in range(kvl) for w in (0, 1)] + [(2, h) for h in range(kvl)]
    for what, h in order:
        for i in range(1, ulysses):
            incoming(what, h, i).start()
        own_in(what, h).start()

    def arrive(what, h):
        own_in(what, h).wait()
        for i in range(1, ulysses):
            incoming(what, h, i).wait_recv()

    ends = []
    starts = []
    total = jnp.int32(0)
    for r in range(reqs):
        starts.append(total)
        total = total + pages_ref[pack, r] * PAGE
        ends.append(total)

    def first_token(pos):
        first = jnp.zeros_like(pos)
        for r in range(reqs):
            first = jnp.maximum(first, jnp.where(pos >= starts[r], starts[r], 0))
        return first

    pos_rows = blk * rows + lax.broadcasted_iota(jnp.int32, (rows, HD), 0)
    rel = (pos_rows - first_token(pos_rows)).astype(jnp.float32)
    angles = rel * freq_ref[...]
    lanes = lax.broadcasted_iota(jnp.int32, (rows, HD), 1)
    cos_t[...] = jnp.cos(angles)
    sine = jnp.sin(angles)
    sin_t[...] = jnp.where(lanes < HD // 2, -sine, sine)

    def onward(which, h, hop):
        tab = (tab_k, tab_v)[which]
        return pltpu.make_async_remote_copy(
            src_ref=tab.at[h, pl.ds(home, rows), :],
            dst_ref=tab.at[h, pl.ds((back - hop) * rows, rows), :],
            send_sem=x_send.at[which, h, hop - 1], recv_sem=x_recv.at[which, h, hop - 1],
            device_id={"blk": lax.rem(blk + hop, blks)}, device_id_type=MESH,
        )

    for h in range(kvl):
        arrive(0, h)
        tab_k[h, pl.ds(home, rows), :] = turn(kraw[h], cos_t[...], sin_t[...])
        arrive(1, h)
        for hop in range(1, back + 1):
            @pl.when(blk + hop < blks)
            def _():
                onward(0, h, hop).start()
                onward(1, h, hop).start()

    def page_for(owner):
        def step(j, found):
            page = table_ref[pack, blk * slots + j]
            return found + jnp.where(lax.div(page, jnp.int32(slots)) == owner, j, 0)
        return lax.fori_loop(0, slots, step, jnp.int32(0))

    def handed(which, i):
        src, dst = ((out_k, got_k), (out_v, got_v))[which]
        return pltpu.make_async_remote_copy(
            src_ref=src.at[i], dst_ref=dst.at[mine],
            send_sem=c_send.at[which, i - 1], recv_sem=c_recv.at[which, i - 1],
            device_id=s_peer(i)[1], device_id_type=MESH,
        )

    def own_page(which):
        src, dst = ((out_k, got_k), (out_v, got_v))[which]
        return pltpu.make_async_copy(src.at[0], dst.at[mine], c_local.at[which])

    for i in range(sources):
        chosen = page_for(s_peer(i)[0])
        for tab, out in ((tab_k, out_k), (tab_v, out_v)):
            out[i] = pick(chosen, [tab[:, home + j * PAGE:home + (j + 1) * PAGE, :] for j in range(slots)])
    for i in range(1, sources):
        handed(0, i).start()
        handed(1, i).start()
    own_page(0).start()
    own_page(1).start()

    block = min(rows, 128)
    lead = min(-(-reach // block) * block, home)
    span = lead + block
    chunk = span if span <= 512 else block
    factor = QUERY_SCALE / SOFT_CAP

    def attend(h, i):
        at = i * block
        if not isinstance(i, int):
            at = pl.multiple_of(at, block)
        here = pl.ds(at, block)
        cosine, sine_here = cos_t[here, :], sin_t[here, :]
        query = jnp.concatenate(
            [turn(qbuf[h, here, g * HD:(g + 1) * HD], cosine, sine_here) for g in range(group)], axis=0
        )
        pos = blk * rows + at + lax.broadcasted_iota(jnp.int32, (block, 1), 0)
        low = jnp.maximum(first_token(pos), pos - (WINDOW - 1))
        pos = jnp.concatenate([pos] * group, axis=0)
        low = jnp.concatenate([low] * group, axis=0)
        begin = home + at - lead

        def part(c):
            start = begin + c * chunk
            if not isinstance(start, int):
                start = pl.multiple_of(start, block)
            seen = pl.ds(start, chunk)
            scores = lax.dot_general(
                query, tab_k[h, seen, :], (((1,), (1,)), ((), ())), preferred_element_type=jnp.float32
            )
            weights = jnp.exp(SOFT_CAP * jnp.tanh(scores * factor))
            key_pos = (blk - back) * rows + start + lax.broadcasted_iota(jnp.int32, (1, chunk), 1)
            weights = jnp.where((key_pos <= pos) & (key_pos >= low), weights, 0.0)
            total = jnp.sum(weights, axis=1, keepdims=True)
            mixed = jnp.dot(
                weights.astype(jnp.bfloat16), tab_v[h, seen, :], preferred_element_type=jnp.float32
            )
            return mixed, total

        if span == chunk:
            mixed, total = part(0)
        else:
            def step(c, carry):
                mixed, total = part(c)
                return carry[0] + mixed, carry[1] + total
            mixed, total = lax.fori_loop(
                0, span // chunk, step,
                (jnp.zeros((group * block, HD), jnp.float32), jnp.zeros((group * block, 1), jnp.float32)),
            )
        result = (mixed / total).astype(jnp.bfloat16)
        for g in range(group):
            obuf[h, here, g * HD:(g + 1) * HD] = result[g * block:(g + 1) * block]

    def outgoing(h, i):
        return pltpu.make_async_remote_copy(
            src_ref=obuf.at[h, pl.ds(pl.multiple_of(u_peer(i) * local, local), local), :],
            dst_ref=out_ref.at[:, pl.ds(pl.multiple_of((me * kvl + h) * qw, qw), qw)],
            send_sem=o_send.at[h, i - 1], recv_sem=o_recv.at[h, i - 1],
            device_id={"ulysses": u_peer(i)}, device_id_type=MESH,
        )

    def own_out(h):
        return pltpu.make_async_copy(
            obuf.at[h, pl.ds(pl.multiple_of(me * local, local), local), :],
            out_ref.at[:, pl.ds(pl.multiple_of((me * kvl + h) * qw, qw), qw)],
            o_local.at[h],
        )

    for h in range(kvl):
        for hop in range(1, back + 1):
            @pl.when(blk >= hop)
            def _():
                onward(0, h, hop).wait_recv()
                onward(1, h, hop).wait_recv()
        arrive(2, h)
        if rows // block <= 4:
            for i in range(rows // block):
                attend(h, i)
        else:
            def each(i, carry):
                attend(h, i)
                return carry
            lax.fori_loop(0, rows // block, each, 0)
        for i in range(1, ulysses):
            outgoing(h, i).start()
        own_out(h).start()

    own_page(0).wait()
    own_page(1).wait()
    for i in range(1, sources):
        handed(0, i).wait_recv()
        handed(1, i).wait_recv()
    for j in range(slots):
        def step(n, found, j=j):
            s = n // slots
            page = table_ref[lax.rem(s, cores), (s // cores) * slots + lax.rem(n, slots)]
            return found + jnp.where(page == mine * slots + j, s, 0)
        source = lax.fori_loop(0, sources * slots, step, jnp.int32(0))
        ck_ref[j] = pick(source, [got_k[s] for s in range(sources)])
        cv_ref[j] = pick(source, [got_v[s] for s in range(sources)])

    for i in range(1, sources):
        handed(0, i).wait_send()
        handed(1, i).wait_send()
    for what, h in order:
        for i in range(1, ulysses):
            incoming(what, h, i).wait_send()
    for h in range(kvl):
        for hop in range(1, back + 1):
            @pl.when(blk + hop < blks)
            def _():
                onward(0, h, hop).wait_send()
                onward(1, h, hop).wait_send()
    for h in range(kvl):
        own_out(h).wait()
        for i in range(1, ulysses):
            outgoing(h, i).wait()


def near_kernel(
    sizes, q_ref, k_ref, v_ref, freq_ref, pages_ref, table_ref,
    out_ref, ck_ref, cv_ref,
    kraw, tab_k, tab_v, qbuf, obuf, cos_t, sin_t, out_k, out_v, got_k, got_v,
    in_send, in_recv, in_local, x_send, x_recv, c_send, c_recv, c_local, o_send, o_recv, o_local,
):
    ulysses, blks, cores, local, kvl, group, reach, reqs = sizes
    rows = ulysses * local
    slots = rows // PAGE
    sources = blks * cores
    back = min(-(-reach // rows), blks - 1)
    home = back * rows
    half = ulysses // 2
    part = half * local
    qw = group * HD
    me = lax.axis_index("ulysses")
    blk = lax.axis_index("blk")
    pack = lax.axis_index("handoff")
    mine = blk * cores + pack
    side = me // half
    member = lax.rem(me, half)
    diagonal = back > 0

    def quarter(a, device):
        return device if a == 0 else lax.rem(device + half, ulysses)

    def h_peer(i):
        return side * half + lax.rem(member + i, half)

    barrier = pltpu.get_barrier_semaphore()

    def u_peer(i):
        return lax.rem(me + i, ulysses)

    def s_peer(i):
        p = lax.rem(mine + i, sources)
        return p, {"blk": p // cores, "handoff": lax.rem(p, cores)}

    for i in range(1, ulysses):
        pl.semaphore_signal(barrier, inc=1, device_id={"ulysses": u_peer(i)}, device_id_type=MESH)
    for i in range(1, sources):
        pl.semaphore_signal(barrier, inc=1, device_id=s_peer(i)[1], device_id_type=MESH)

    if diagonal:
        @pl.when((side == 0) & (blk > 0))
        def _():
            pl.semaphore_signal(
                barrier, inc=1, device_id={"blk": lax.rem(blk + blks - 1, blks), "ulysses": quarter(1, me)},
                device_id_type=MESH,
            )

    for hop in range(1, back + 1):
        @pl.when(blk < hop)
        def _():
            gap = pl.ds((back - hop) * rows, rows)
            tab_k[:, :, gap, :] = jnp.zeros((2, kvl, rows, HD), jnp.bfloat16)
            tab_v[:, :, gap, :] = jnp.zeros((2, kvl, rows, HD), jnp.bfloat16)

    greeted = ulysses - 1 + sources - 1
    if diagonal:
        awaited = (side == 1) & (blk + 1 < blks)

        @pl.when(awaited)
        def _():
            pl.semaphore_wait(barrier, greeted + 1)

        @pl.when(jnp.logical_not(awaited))
        def _():
            pl.semaphore_wait(barrier, greeted)
    else:
        pl.semaphore_wait(barrier, greeted)

    def landing(what, a, h, whose):
        if what == 0:
            return kraw.at[a, h, pl.ds(whose * local, local), :]
        if what == 1:
            return tab_v.at[a, h, pl.ds(home + whose * local, local), :]
        return qbuf.at[a, h, pl.ds(lax.rem(whose, half) * local, local), :]

    def leaving(what, a, h, whose):
        width = qw if what == 2 else HD
        ref = (k_ref, v_ref, q_ref)[what]
        return ref.at[:, pl.ds(pl.multiple_of((quarter(a, whose) * kvl + h) * width, width), width)]

    def incoming(what, a, h, i):
        peer = h_peer(i) if what == 2 else u_peer(i)
        return pltpu.make_async_remote_copy(
            src_ref=leaving(what, a, h, peer), dst_ref=landing(what, a, h, me),
            send_sem=in_send.at[what, a, h, i - 1], recv_sem=in_recv.at[what, a, h, i - 1],
            device_id={"ulysses": peer}, device_id_type=MESH,
        )

    def own_in(what, a, h):
        return pltpu.make_async_copy(
            leaving(what, a, h, me), landing(what, a, h, me), in_local.at[what, a, h]
        )

    def each_send(what, a, act):
        for i in range(1, half if what == 2 else ulysses):
            if what == 2 or a == 0:
                act(i)
            else:
                @pl.when(u_peer(i) // half >= side)
                def _(i=i):
                    act(i)

    def each_receive(what, a, act):
        for i in range(1, half if what == 2 else ulysses):
            if what == 2 or a == 0:
                act(i)
            else:
                @pl.when(lax.rem(me + ulysses - i, ulysses) // half <= side)
                def _(i=i):
                    act(i)

    order = []
    for a in (0, 1):
        order += [(w, a, h) for h in range(kvl) for w in (0, 1)]
        order += [(2, a, h) for h in range(kvl)]
    for what, a, h in order:
        each_send(what, a, lambda i, what=what, a=a, h=h: incoming(what, a, h, i).start())
        own_in(what, a, h).start()

    def arrive(what, a, h):
        own_in(what, a, h).wait()
        each_receive(what, a, lambda i: incoming(what, a, h, i).wait_recv())

    ends = []
    starts = []
    total = jnp.int32(0)
    for r in range(reqs):
        starts.append(total)
        total = total + pages_ref[pack, r] * PAGE
        ends.append(total)

    def first_token(pos):
        first = jnp.zeros_like(pos)
        for r in range(reqs):
            first = jnp.maximum(first, jnp.where(pos >= starts[r], starts[r], 0))
        return first

    pos_rows = blk * rows + lax.broadcasted_iota(jnp.int32, (rows, HD), 0)
    rel = (pos_rows - first_token(pos_rows)).astype(jnp.float32)
    angles = rel * freq_ref[...]
    lanes = lax.broadcasted_iota(jnp.int32, (rows, HD), 1)
    cos_t[...] = jnp.cos(angles)
    sine = jnp.sin(angles)
    sin_t[...] = jnp.where(lanes < HD // 2, -sine, sine)

    def onward(kind, which, h):
        tab = (tab_k, tab_v)[which]
        begin, length = (0, rows) if kind == 0 else (side * part, part)
        source = 1 if kind == 1 else 0
        target = 0 if kind == 0 else 1
        device = {"blk": lax.rem(blk + 1, blks)}
        if kind == 2:
            device["ulysses"] = quarter(1, me)
            begin = part
        return pltpu.make_async_remote_copy(
            src_ref=tab.at[source, h, pl.ds(home + begin, length), :],
            dst_ref=tab.at[target, h, pl.ds(begin, length), :],
            send_sem=x_send.at[kind, which, h], recv_sem=x_recv.at[kind, which, h],
            device_id=device, device_id_type=MESH,
        )

    def intake(a):
        for h in range(kvl):
            arrive(0, a, h)
            first = rows if a == 0 else part
            tab_k[a, h, pl.ds(home, first), :] = turn(
                kraw[a, h, pl.ds(0, first), :], cos_t[pl.ds(0, first), :], sin_t[pl.ds(0, first), :]
            )
            if a == 1:
                @pl.when(side == 1)
                def _(h=h):
                    rest = pl.ds(part, part)
                    tab_k[1, h, pl.ds(home + part, part), :] = turn(
                        kraw[1, h, rest, :], cos_t[rest, :], sin_t[rest, :]
                    )
            arrive(1, a, h)
            if diagonal:
                @pl.when(blk + 1 < blks)
                def _(a=a, h=h):
                    onward(a, 0, h).start()
                    onward(a, 1, h).start()
                if a == 0:
                    @pl.when((blk + 1 < blks) & (side == 1))
                    def _(h=h):
                        onward(2, 0, h).start()
                        onward(2, 1, h).start()

    intake(0)

    def page_for(owner):
        def step(j, found):
            page = table_ref[pack, blk * slots + j]
            return found + jnp.where(lax.div(page, jnp.int32(slots)) == owner, j, 0)
        return lax.fori_loop(0, slots, step, jnp.int32(0))

    def handed(which, i):
        src, dst = ((out_k, got_k), (out_v, got_v))[which]
        return pltpu.make_async_remote_copy(
            src_ref=src.at[i], dst_ref=dst.at[mine],
            send_sem=c_send.at[which, i - 1], recv_sem=c_recv.at[which, i - 1],
            device_id=s_peer(i)[1], device_id_type=MESH,
        )

    def own_page(which):
        src, dst = ((out_k, got_k), (out_v, got_v))[which]
        return pltpu.make_async_copy(src.at[0], dst.at[mine], c_local.at[which])

    for i in range(sources):
        chosen = page_for(s_peer(i)[0])
        for tab, out in ((tab_k, out_k), (tab_v, out_v)):
            out[i] = pick(chosen, [tab[0, :, home + j * PAGE:home + (j + 1) * PAGE, :] for j in range(slots)])
    for i in range(1, sources):
        handed(0, i).start()
        handed(1, i).start()
    own_page(0).start()
    own_page(1).start()

    block = part
    lead = min(-(-reach // block) * block, home)
    span = lead + block
    chunk = span
    factor = QUERY_SCALE / SOFT_CAP

    def attend(a, h, at):
        here = pl.ds(at, block)
        cosine, sine_here = cos_t[here, :], sin_t[here, :]
        query = jnp.concatenate(
            [turn(qbuf[a, h, :, g * HD:(g + 1) * HD], cosine, sine_here) for g in range(group)], axis=0
        )
        pos = blk * rows + at + lax.broadcasted_iota(jnp.int32, (block, 1), 0)
        low = jnp.maximum(first_token(pos), pos - (WINDOW - 1))
        pos = jnp.concatenate([pos] * group, axis=0)
        low = jnp.concatenate([low] * group, axis=0)
        begin = home + at - lead

        def piece():
            start = begin
            seen = pl.ds(start, chunk)
            scores = lax.dot_general(
                query, tab_k[a, h, seen, :], (((1,), (1,)), ((), ())), preferred_element_type=jnp.float32
            )
            weights = jnp.exp(SOFT_CAP * jnp.tanh(scores * factor))
            key_pos = (blk - back) * rows + start + lax.broadcasted_iota(jnp.int32, (1, chunk), 1)
            weights = jnp.where((key_pos <= pos) & (key_pos >= low), weights, 0.0)
            total = jnp.sum(weights, axis=1, keepdims=True)
            mixed = jnp.dot(
                weights.astype(jnp.bfloat16), tab_v[a, h, seen, :], preferred_element_type=jnp.float32
            )
            return mixed, total

        mixed, total = piece()
        result = (mixed / total).astype(jnp.bfloat16)
        for g in range(group):
            obuf[a, h, :, g * HD:(g + 1) * HD] = result[g * block:(g + 1) * block]

    def columns(a, h):
        return out_ref.at[:, pl.ds(pl.multiple_of((quarter(a, me) * kvl + h) * qw, qw), qw)]

    def finished(a, h, device):
        start = pl.multiple_of(lax.rem(device, half) * local, local)
        return obuf.at[a, h, pl.ds(start, local), :]

    def outgoing(a, h, i):
        return pltpu.make_async_remote_copy(
            src_ref=finished(a, h, h_peer(i)), dst_ref=columns(a, h),
            send_sem=o_send.at[a, h, i - 1], recv_sem=o_recv.at[a, h, i - 1],
            device_id={"ulysses": h_peer(i)}, device_id_type=MESH,
        )

    def own_out(a, h):
        return pltpu.make_async_copy(finished(a, h, me), columns(a, h), o_local.at[a, h])

    def heads(a):
        for h in range(kvl):
            if diagonal:
                @pl.when(blk > 0)
                def _(a=a, h=h):
                    onward(a, 0, h).wait_recv()
                    onward(a, 1, h).wait_recv()
                if a == 1:
                    @pl.when((blk > 0) & (side == 0))
                    def _(h=h):
                        onward(2, 0, h).wait_recv()
                        onward(2, 1, h).wait_recv()
            arrive(2, a, h)
            for where in (0, 1):
                @pl.when(side == where)
                def _(a=a, h=h, where=where):
                    attend(a, h, where * part)
            for i in range(1, half):
                outgoing(a, h, i).start()
            own_out(a, h).start()

    heads(0)
    intake(1)
    heads(1)

    own_page(0).wait()
    own_page(1).wait()
    for i in range(1, sources):
        handed(0, i).wait_recv()
        handed(1, i).wait_recv()
    for j in range(slots):
        def step(n, found, j=j):
            s = n // slots
            page = table_ref[lax.rem(s, cores), (s // cores) * slots + lax.rem(n, slots)]
            return found + jnp.where(page == mine * slots + j, s, 0)
        source = lax.fori_loop(0, sources * slots, step, jnp.int32(0))
        ck_ref[j] = pick(source, [got_k[s] for s in range(sources)])
        cv_ref[j] = pick(source, [got_v[s] for s in range(sources)])

    for i in range(1, sources):
        handed(0, i).wait_send()
        handed(1, i).wait_send()
    for what, a, h in order:
        each_send(what, a, lambda i, what=what, a=a, h=h: incoming(what, a, h, i).wait_send())
    for h in range(kvl):
        if diagonal:
            @pl.when(blk + 1 < blks)
            def _(h=h):
                for kind in (0, 1):
                    onward(kind, 0, h).wait_send()
                    onward(kind, 1, h).wait_send()

            @pl.when((blk + 1 < blks) & (side == 1))
            def _(h=h):
                onward(2, 0, h).wait_send()
                onward(2, 1, h).wait_send()
    for a in (0, 1):
        for h in range(kvl):
            own_out(a, h).wait()
            for i in range(1, half):
                outgoing(a, h, i).wait()


def place(*refs):
    count = (len(refs) - 1) // 2
    sem = refs[-1]
    copies = [pltpu.make_async_copy(refs[i], refs[count + i], sem.at[i]) for i in range(count)]
    for copy in copies:
        copy.start()
    for copy in copies:
        copy.wait()


def body(queries, keys, values, request_pages, page_table):
    local = queries.shape[1]
    ulysses = lax.axis_size("ulysses")
    blks = lax.axis_size("blk")
    cores = lax.axis_size("handoff")
    kvl = KVH // ulysses
    group = QH // KVH
    rows = local * ulysses
    slots = rows // PAGE
    sources = blks * cores
    assert slots == sources
    reach = min(WINDOW, page_table.shape[1] // 2 * PAGE)
    back = min(-(-reach // rows), blks - 1)
    reqs = request_pages.shape[1]
    half = np.arange(HD // 2, dtype=np.float64)
    freq = (ROPE_BASE ** (-2.0 * half / HD)).astype(np.float32)
    freq = jnp.asarray(np.concatenate([freq, freq])[None, :])
    sizes = (ulysses, blks, cores, local, kvl, group, reach, reqs)
    qw = group * HD
    bf = jnp.bfloat16
    dma = pltpu.SemaphoreType.DMA
    hops = max(back, 1)
    near = reach <= rows and ulysses % 2 == 0 and ulysses > 2
    sets = (2,) if near else ()
    mates = (ulysses // 2 if near else ulysses) - 1
    asked = mates + 1 if near else ulysses
    anywhere = pl.BlockSpec(memory_space=pl.ANY)
    vmem = pl.BlockSpec(memory_space=pltpu.VMEM)
    smem = pl.BlockSpec(memory_space=pltpu.SMEM)
    results = pl.pallas_call(
        functools.partial(near_kernel if near else kernel, sizes),
        out_shape=(
            pltpu.VMEM((local, QH * HD), bf),
            pltpu.VMEM((slots, kvl, PAGE, HD), bf),
            pltpu.VMEM((slots, kvl, PAGE, HD), bf),
        ),
        in_specs=[anywhere, anywhere, anywhere, vmem, smem, smem],
        out_specs=(vmem, vmem, vmem),
        scratch_shapes=[
            pltpu.VMEM(sets + (kvl, rows, HD), bf),
            pltpu.VMEM(sets + (kvl, (back + 1) * rows, HD), bf),
            pltpu.VMEM(sets + (kvl, (back + 1) * rows, HD), bf),
            pltpu.VMEM(sets + (kvl, asked * local, qw), bf),
            pltpu.VMEM(sets + (kvl, asked * local, qw), bf),
            pltpu.VMEM((rows, HD), jnp.float32),
            pltpu.VMEM((rows, HD), jnp.float32),
            pltpu.VMEM((sources, kvl, PAGE, HD), bf),
            pltpu.VMEM((sources, kvl, PAGE, HD), bf),
            pltpu.VMEM((sources, kvl, PAGE, HD), bf),
            pltpu.VMEM((sources, kvl, PAGE, HD), bf),
            dma((3,) + sets + (kvl, ulysses - 1)),
            dma((3,) + sets + (kvl, ulysses - 1)),
            dma((3,) + sets + (kvl,)),
            dma((3, 2, kvl) if near else (2, kvl, hops)),
            dma((3, 2, kvl) if near else (2, kvl, hops)),
            dma((2, sources - 1)),
            dma((2, sources - 1)),
            dma((2,)),
            dma(sets + (kvl, mates)),
            dma(sets + (kvl, mates)),
            dma(sets + (kvl,)),
        ],
        compiler_params=pltpu.CompilerParams(collective_id=1 if near else 0, has_side_effects=True),
    )(queries[0], keys[0], values[0], freq, request_pages, page_table)
    results = [pltpu.with_memory_space_constraint(x, pltpu.VMEM) for x in results]
    attended, cache_keys, cache_values = pl.pallas_call(
        place,
        out_shape=tuple(jax.ShapeDtypeStruct(x.shape, x.dtype) for x in results),
        in_specs=[anywhere] * len(results),
        out_specs=(anywhere,) * len(results),
        scratch_shapes=[dma((len(results),))],
        compiler_params=pltpu.CompilerParams(vmem_limit_bytes=1 << 20),
    )(*results)
    return (attended[None], cache_keys, cache_values)


def solution(mesh):
    in_specs = (
        P(("groups", "handoff"), ("blk", "ulysses"), None),
        P(("groups", "handoff"), ("blk", "ulysses"), None),
        P(("groups", "handoff"), ("blk", "ulysses"), None),
        P("groups", None),
        P("groups", None),
    )
    out_specs = (
        P(("groups", "handoff"), ("blk", "ulysses"), None),
        P(("groups", "blk", "handoff"), "ulysses", None, None),
        P(("groups", "blk", "handoff"), "ulysses", None, None),
    )
    return jax.shard_map(body, mesh=mesh, in_specs=in_specs, out_specs=out_specs, check_vma=False)
```
